256 devices in a mesh: lat: 64 (over x, y_lo, z), coh: 4 (over y_hi, core).
Axes of the slice: x: 4, y: 4 (y_hi: 2, y_lo: 2; y = y_hi * 2 + y_lo), z: 8, core: 2. Of those that a mesh axis runs over, the one named last changes fastest.
Arguments:
- density: float32 [128, 2, 512, 1024], P('coh', None, 'lat'), may hold values from 0.1 to 1
- cotangent: float32 [128, 2, 512, 1024], P('coh', None, 'lat'), may hold values from -0.5 to 1.5
- land_mask: int32 [2, 512, 1024], P(None, 'lat'), may hold values 0 or 1
- east_vel: float32 [2, 512, 1024], P(None, 'lat'), may hold values from -0.4 to 0.4
- north_vel: float32 [2, 512, 1024], P(None, 'lat'), may hold values from -0.4 to 0.4
- diffusion: float32 [2, 512, 1024], P(None, 'lat'), may hold values from 0.02 to 0.2
- age_class: int32 [128], P('coh'), may hold values from 0 to 31, as said below
- mort_rate: float32 [32], replicated, may hold values from 0.05 to 0.5
- crowd_coef: float32 [32], replicated, may hold values from 1 to 4
- mass: float32 [32], replicated, may hold values from 0.5 to 2
- speed: float32 [32], replicated, may hold values from 0.25 to 1
Outputs:
- grad_density: float32 [128, 2, 512, 1024], P('coh', None, 'lat')
- grad_east_vel: float32 [2, 512, 1024], P(None, 'lat', 'coh')
- grad_north_vel: float32 [2, 512, 1024], P(None, 'lat', 'coh')
- grad_diffusion: float32 [2, 512, 1024], P(None, 'lat', 'coh')
The draws below stay inside these ranges and needn't reach their ends.
Inputs may be any that keep to these rules, and one draw needn't show every extreme that they name: `age_class`: each age class is held by exactly 4 cohorts.
All inputs are finite; a program needn't handle non-finite values. No bound on the sum of `land_mask` on one device may be relied on, other than what follows from the above.
Results may differ from the reference program's by a relative error of at most 0.00014.
Values sent between devices are 32-bit elements; how exact they have to be, the bound alone decides.
No kernel may reach another device: no remote copies, remote signals or barrier semaphores. Data moves between devices by JAX's collectives and lax.ppermute only.
A program may use at most 128 MiB of HBM per device.

```python
import math
import jax
import jax.numpy as jnp
from jax import lax

COH = 128
NAGE = 32
LAYERS = 2
STEPS = 2
LON = 1024
LAT = 512


def draw_age_class(key, part):
    shuffled = jax.random.permutation(key, COH)
    return (shuffled % NAGE).astype(jnp.int32)


def plant(values, stream_key, low, largest):
    longest = values.shape.index(max(values.shape))
    spots = []
    for shift in (0, 1):
        where = [jax.random.randint(jax.random.fold_in(stream_key, axis), (), 0, length) for axis, length in enumerate(values.shape)]
        where[longest] = (where[longest] + shift) % values.shape[longest]
        spots.append(tuple(where))
    return values.at[spots[0]].set(low).at[spots[1]].set(largest)


def level_of(rng, dims, split, smallest, largest):
    def one(position, shards_of):
        heights = jax.random.uniform(jax.random.fold_in(jax.random.fold_in(rng, 6), position), (shards_of,), jnp.float32, smallest / len(split), largest / len(split))
        return jnp.repeat(jnp.exp(heights), dims[position] // shards_of).reshape((-1,) + (1,) * (len(dims) - position - 1))

    level = one(*split[0])
    for cut in split[1:]:
        level = level * one(*cut)
    return level


def setup_inputs(seed: int = 0) -> dict:
    seeds = jax.random.split(jax.random.key(seed), 12)
    return {
        "density": jnp.clip(jnp.exp(math.log(1.0) - 2.3025851 * jax.random.uniform(seeds[0], (COH, LAYERS, LAT, LON), jnp.float32) ** level_of(seeds[0], (COH, LAYERS, LAT, LON), ((0, 4), (2, 64)), -0.2, 0.2)), 0.1, 1.0),
        "cotangent": jnp.clip(-0.5 + 2.0 * jax.random.uniform(seeds[1], (COH, LAYERS, LAT, LON), jnp.float32) ** level_of(seeds[1], (COH, LAYERS, LAT, LON), ((0, 4), (2, 64)), -0.2, 0.2), -0.5, 1.5),
        "land_mask": plant((jax.random.randint(seeds[2], (LAYERS, LAT, LON), 0, 8) < 7).astype(jnp.int32), jax.random.fold_in(seeds[2], 1), 0, 1),
        "east_vel": jnp.clip(jax.random.uniform(seeds[3], (LAYERS, LAT, LON), jnp.float32, -0.4, 0.4) * level_of(seeds[3], (LAYERS, LAT, LON), ((1, 64),), -0.4, 0.0), -0.4, 0.4),
        "north_vel": jnp.clip(jax.random.uniform(seeds[4], (LAYERS, LAT, LON), jnp.float32, -0.4, 0.4) * level_of(seeds[4], (LAYERS, LAT, LON), ((1, 64),), -0.4, 0.0), -0.4, 0.4),
        "diffusion": jnp.clip(0.02 + 0.18 * jax.random.uniform(seeds[5], (LAYERS, LAT, LON), jnp.float32) ** level_of(seeds[5], (LAYERS, LAT, LON), ((1, 64),), -0.2, 0.2), 0.02, 0.2),
        "age_class": draw_age_class(jax.random.fold_in(seeds[11], 71), 0),
        "mort_rate": jnp.clip(jnp.exp(jax.random.uniform(seeds[7], (NAGE,), jnp.float32, math.log(0.05), math.log(0.5))), 0.05, 0.5),
        "crowd_coef": jnp.clip(jnp.exp(jax.random.uniform(seeds[8], (NAGE,), jnp.float32, math.log(1.0), math.log(4.0))), 1.0, 4.0),
        "mass": jnp.clip(jnp.exp(jax.random.uniform(seeds[9], (NAGE,), jnp.float32, math.log(0.5), math.log(2.0))), 0.5, 2.0),
        "speed": jnp.clip(jnp.exp(jax.random.uniform(seeds[10], (NAGE,), jnp.float32, math.log(0.25), math.log(1.0))), 0.25, 1.0),
    }


def advance(state, ocean, east_vel, north_vel, diffusion, mortal, crowding, weight, swim):
    crowd = lax.optimization_barrier(jnp.sum(weight * state, axis=0)) / COH
    survival = jnp.exp(-(mortal + crowding * crowd[None]))
    survived = state * survival
    wet = ocean[None] * survived
    zero_row = jnp.zeros_like(wet[:, :, :1])
    north_val = jnp.concatenate([wet[:, :, 1:], zero_row], axis=2)
    south_val = jnp.concatenate([zero_row, wet[:, :, :-1]], axis=2)
    east_val = jnp.roll(wet, -1, axis=3)
    west_val = jnp.roll(wet, 1, axis=3)
    laplace = north_val + south_val + east_val + west_val - 4.0 * wet
    east_diff = 0.5 * (east_val - west_val)
    north_diff = 0.5 * (north_val - south_val)
    east_coef = swim * east_vel[None]
    north_coef = swim * north_vel[None]
    return ocean[None] * (wet + diffusion[None] * laplace - east_coef * east_diff - north_coef * north_diff)

def reference(density, cotangent, land_mask, east_vel, north_vel, diffusion, age_class, mort_rate, crowd_coef, mass, speed):
    ocean = land_mask.astype(density.dtype)
    mortal = mort_rate[age_class][:, None, None, None]
    crowding = crowd_coef[age_class][:, None, None, None]
    weight = mass[age_class][:, None, None, None]
    swim = speed[age_class][:, None, None, None]

    def forward(start, east_field, north_field, diff_field):

        def single(state):
            return advance(state, ocean, east_field, north_field, diff_field, mortal, crowding, weight, swim)
        stepper = jax.checkpoint(single)
        state = start
        for section in range(STEPS):
            state = stepper(state)
        return state
    final, pull = jax.vjp(forward, density, east_vel, north_vel, diffusion)
    grads = pull(cotangent)
    return (grads[0], grads[1], grads[2], grads[3])
```

```python
import jax
import jax.numpy as jnp
from jax import lax
from jax.sharding import PartitionSpec as P

COH = 128
STEPS = 2


def extended(value, sides, width):
    for axis, dim in sides:
        devices, length = (lax.axis_size(axis), value.shape[dim])
        up = [(i, (i + 1) % devices) for i in range(devices - 1)]
        down = [(j, i) for i, j in up]
        last = lax.slice_in_dim(value, length - width, length, axis=dim)
        first = lax.slice_in_dim(value, 0, width, axis=dim)
        before = lax.ppermute(last, axis, up)
        after = lax.ppermute(first, axis, down)
        value = jnp.concatenate([before, value, after], axis=dim)
    return value


def swap(value, flip):
    return lax.ppermute(value, "coh", [(i, i ^ flip) for i in range(4)])


def total(value):
    value = value + swap(value, 1)
    return value + swap(value, 2)


def scatter(value):
    high, low = lax.axis_index("coh") // 2, lax.axis_index("coh") % 2
    split = value.reshape(value.shape[:-1] + (2, 2, value.shape[-1] // 4))

    def halves(array, dim, side):
        first, second = (lax.index_in_dim(array, k, dim, keepdims=False) for k in range(2))
        return jnp.where(side == 0, first, second), jnp.where(side == 0, second, first)

    keep, send = halves(split, split.ndim - 2, low)
    keep, send = halves(keep + swap(send, 1), keep.ndim - 2, high)
    return keep + swap(send, 2)


def rows(value, up):
    devices, length = (lax.axis_size("lat"), value.shape[2])
    edge = lax.slice_in_dim(value, length - 1, length, axis=2) if up else lax.slice_in_dim(value, 0, 1, axis=2)
    pairs = [(i, i + 1) if up else (i + 1, i) for i in range(devices - 1)]
    return lax.ppermute(edge, "lat", pairs)


def lookup(age_class, mort_rate, crowd_coef, mass, speed):
    classes = jnp.arange(mort_rate.shape[0], dtype=jnp.int32)
    onehot = (age_class[:, None] == classes[None, :]).astype(jnp.float32)
    tables = jnp.stack([mort_rate, crowd_coef, mass, speed], axis=1)
    picked = jnp.dot(onehot, tables, precision=lax.Precision.HIGHEST)
    return [picked[:, column][:, None, None, None] for column in range(4)]


def local(
    density,
    cotangent,
    land_mask,
    east_vel,
    north_vel,
    diffusion,
    age_class,
    mort_rate,
    crowd_coef,
    mass,
    speed,
):
    ocean = land_mask.astype(jnp.float32)[None]
    mortal, crowding, weight, swim = lookup(age_class, mort_rate, crowd_coef, mass, speed)
    east_coef = swim * east_vel[None]
    north_coef = swim * north_vel[None]
    kappa = diffusion[None]
    state = density
    saved = []
    for section in range(STEPS):
        crowd = total(jnp.sum(weight * state, axis=0)) / COH
        survival = jnp.exp(-(mortal + crowding * crowd[None]))
        survived = state * survival
        wet = ocean * survived
        padded = extended(wet, (("lat", 2),), 1)
        north_val = padded[:, :, 2:]
        south_val = padded[:, :, :-2]
        east_val = jnp.roll(wet, -1, axis=3)
        west_val = jnp.roll(wet, 1, axis=3)
        laplace = north_val + south_val + east_val + west_val - 4.0 * wet
        east_diff = 0.5 * (east_val - west_val)
        north_diff = 0.5 * (north_val - south_val)
        state = ocean * (wet + kappa * laplace - east_coef * east_diff - north_coef * north_diff)
        saved.append((survival, survived, laplace, east_diff, north_diff))
    adjoint = cotangent
    shares = None
    for section in reversed(range(STEPS)):
        survival, survived, laplace, east_diff, north_diff = saved[section]
        masked = ocean * adjoint
        grad_east = -jnp.sum(masked * swim * east_diff, axis=0)
        grad_north = -jnp.sum(masked * swim * north_diff, axis=0)
        grad_kappa = jnp.sum(masked * laplace, axis=0)
        pieces = jnp.stack([grad_east, grad_north, grad_kappa])
        shares = pieces if shares is None else shares + pieces
        to_north = (kappa - 0.5 * north_coef) * masked
        to_south = (kappa + 0.5 * north_coef) * masked
        to_east = (kappa - 0.5 * east_coef) * masked
        to_west = (kappa + 0.5 * east_coef) * masked
        from_below = jnp.concatenate([rows(to_north, True), to_north[:, :, :-1]], axis=2)
        from_above = jnp.concatenate([to_south[:, :, 1:], rows(to_south, False)], axis=2)
        grad_wet = (
            (1.0 - 4.0 * kappa) * masked
            + jnp.roll(to_east, 1, axis=3)
            + jnp.roll(to_west, -1, axis=3)
            + from_below
            + from_above
        )
        grad_surv = ocean * grad_wet
        pressure = total(jnp.sum(-crowding * grad_surv * survived, axis=0))
        adjoint = grad_surv * survival + weight / COH * pressure[None]
    shares = scatter(shares)
    return (adjoint, shares[0], shares[1], shares[2])


def solution(mesh):
    in_specs = (
        P("coh", None, "lat", None),
        P("coh", None, "lat", None),
        P(None, "lat", None),
        P(None, "lat", None),
        P(None, "lat", None),
        P(None, "lat", None),
        P("coh"),
        P(),
        P(),
        P(),
        P(),
    )
    out_specs = (
        P("coh", None, "lat", None),
        P(None, "lat", "coh"),
        P(None, "lat", "coh"),
        P(None, "lat", "coh"),
    )
    return jax.shard_map(local, mesh=mesh, in_specs=in_specs, out_specs=out_specs, check_vma=False)
```

```python
import functools

import jax
import jax.numpy as jnp
from jax import lax
from jax.experimental import pallas as pl
from jax.experimental.pallas import tpu as pltpu
from jax.sharding import PartitionSpec as P


COH = 128
LOG2E = 1.4426950408889634
STEP = 4
F32 = jnp.float32


def rows_of(shape):
    return lax.broadcasted_iota(jnp.int32, shape, 0)


def turn(tile, shift):
    return pltpu.roll(tile, shift, 0)


def east(tile):
    return pltpu.roll(tile, tile.shape[1] - 1, 1)


def west(tile):
    return pltpu.roll(tile, 1, 1)


def northern(first, second, halo):
    row = rows_of(first.shape)
    return (
        jnp.where(row == 7, turn(halo, 3), turn(first, 7)),
        jnp.where(row == 7, turn(halo, 1), turn(second, 7)),
    )


def southern(first, second, halo):
    row = rows_of(first.shape)
    return (
        jnp.where(row == 0, turn(halo, 7), turn(first, 1)),
        jnp.where(row == 0, turn(halo, 5), turn(second, 1)),
    )


def within(tile, shift):
    return jnp.where(rows_of(tile.shape) == (0 if shift == 1 else 7), 0.0, turn(tile, shift))


def rim(first, second):
    row = rows_of(first.shape)
    last = jnp.where(row == 4, turn(first, 5), turn(second, 7))
    return jnp.where(row == 1, turn(first, 1), jnp.where(row == 3, turn(second, 3), last))


def halo_neighbours(own, north, south):
    row = rows_of(own.shape)
    lower, upper = (row == 1) | (row == 3), (row == 4) | (row == 6)
    return jnp.where(lower, own, turn(north, 7)), jnp.where(upper, own, turn(south, 1))


def combine(inner, added):
    row = rows_of(inner.shape)
    used = (row == 1) | (row == 3) | (row == 4) | (row == 6)
    return jnp.where(used, inner, jnp.where(row < 4, turn(added, 7), turn(added, 1)))


def addends(both):
    row = rows_of(both.shape)
    return (
        jnp.where(row == 0, both, jnp.where(row == 7, turn(both, 2), 0.0)),
        jnp.where(row == 7, both, jnp.where(row == 0, turn(both, 6), 0.0)),
    )


def stay(value):
    return pltpu.with_memory_space_constraint(value, pltpu.HBM)


def decays(mortal, crowded, crowd):
    return jnp.exp2(-LOG2E * mortal - (LOG2E / COH * crowded) * crowd)


def join(before, after, out):
    out[0:4, :] = before
    out[4:8, :] = after


def pack(source, up, down, slot):
    for out, start in ((up, 6), (down, 0)):
        out[slot, 0:2, :] = source(0, start)
        out[slot, 2:4, :] = source(1, start)


def clear(*refs):
    for ref in refs:
        ref[...] = jnp.zeros_like(ref)


def nothing():
    pass


def crowd_kernel(age, mass, state, crowd):
    def begin():
        clear(crowd)

    def each(group):
        for layer in range(2):
            crowd[layer] += sum(mass[age[c]] * state[c, layer] for c in group)

    return begin, each, nothing


def edges_kernel(*refs):
    *raw, state, up, down = refs

    def begin():
        for slot, field in enumerate(raw):
            pack(lambda layer, start: field[layer, start : start + 2, :].astype(F32), up, down, state.shape[0] + slot)
        if raw:
            for out in (up, down):
                out[state.shape[0] + len(raw)] = jnp.zeros(out.shape[1:], F32)

    def each(group):
        for c in group:
            pack(lambda layer, start: state[c, layer, start : start + 2, :], up, down, c)

    return begin, each, nothing


def forward_kernel(age, mort, crowding, mass, speed, ocean, east_vel, north_vel, kappa, crowd, state,
                   state_out, rims, fields, total, sums, coef):
    def begin():
        clear(total, sums)
        for slot, (field, scale) in enumerate(((ocean, None), (east_vel, 0.5), (north_vel, 0.5), (kappa, None))):
            for layer in range(2):
                fields[slot, layer] = field[layer].astype(F32)
            if scale is not None:
                fields[slot] = scale * fields[slot]
        coef[0] = fields[0] * (1.0 - 4.0 * fields[3])
        coef[1] = fields[0] * fields[3]
        coef[2] = fields[0] * fields[1]
        coef[3] = fields[0] * fields[2]

    def each(group):
        for c in group:
            mortal, crowded, weight, swim = [table[age[c]] for table in (mort, crowding, mass, speed)]
            wet = [state[c, k] * (fields[0, k] * decays(mortal, crowded, crowd[k])) for k in range(2)]
            rims[c] = rim(*wet)
            for k in range(2):
                north, south, to_east, to_west = within(wet[k], 7), within(wet[k], 1), east(wet[k]), west(wet[k])
                around = (north + south) + (to_east + to_west)
                drift = coef[2, k] * (to_east - to_west) + coef[3, k] * (north - south)
                moved = coef[0, k] * wet[k] + coef[1, k] * around - swim * drift
                state_out[c, k] = moved
                total[k] += weight * moved
                mine = weight * wet[k]
                swum = swim * mine
                sums[0, k] += mine
                sums[1, k] += swum
                sums[2, k] += crowded * mine
                sums[3, k] += crowded * swum

    return begin, each, nothing


def forward_halo_kernel(age, mort, crowding, mass, speed, fields, total, before, after, rims,
                        both_out, wet_out, halo_fields, total_out, sums, coef, own, crowd, edge, added):
    def begin():
        clear(sums, added)
        cohorts = rims.shape[0]
        for slot, scale in enumerate((None, 0.5, 0.5, None)):
            join(before[cohorts + slot], after[cohorts + slot], edge.at[0])
            halo_fields[slot] = edge[0] if scale is None else scale * edge[0]
        ocean = halo_fields[0]
        coef[0] = ocean * (1.0 - 4.0 * halo_fields[3])
        coef[1] = ocean * halo_fields[3]
        coef[2] = ocean * halo_fields[1]
        coef[3] = ocean * halo_fields[2]
        row = rows_of(ocean.shape)
        ocean = rim(fields[0, 0], fields[0, 1])
        own[0] = ocean * rim(fields[3, 0], fields[3, 1])
        own[1] = jnp.where(row < 4, ocean, -ocean) * rim(fields[2, 0], fields[2, 1])
        join(before[cohorts + 4], after[cohorts + 4], crowd)

    def each(group):
        for slot, c in enumerate(group):
            join(before[c], after[c], edge.at[slot])
        for slot, c in enumerate(group):
            mortal, crowded, weight, swim = [table[age[c]] for table in (mort, crowding, mass, speed)]
            wet = edge[slot] * (halo_fields[0] * decays(mortal, crowded, crowd[...]))
            wet_out[c] = wet
            north, south = halo_neighbours(rims[c], wet, wet)
            to_east, to_west = east(wet), west(wet)
            around = (north + south) + (to_east + to_west)
            drift = coef[2] * (to_east - to_west) + coef[3] * (north - south)
            moved = coef[0] * wet + coef[1] * around - swim * drift
            both = combine(moved, (own[0] + swim * own[1]) * wet)
            both_out[c] = both
            added[...] += weight * both
            mine = weight * wet
            sums[0] += mine
            sums[1] += swim * mine

    def end():
        total_out[2] = added[...]
        for k, more in enumerate(addends(added[...])):
            total_out[k] = total[k] + more

    return begin, each, end


def transport_coef(fields, coef):
    coef[0] = 1.0 - 4.0 * fields[3]
    coef[1] = fields[3]
    coef[2] = fields[1]
    coef[3] = fields[2]


def pull_kernel(age, speed, fields, cotangent, pulled, rims, coef):
    def begin():
        transport_coef(fields, coef)

    def each(group):
        for c in group:
            swim = speed[age[c]]
            masked = [fields[0, k] * cotangent[c, k] for k in range(2)]
            rims[c] = rim(*masked)
            for k in range(2):
                plain = coef[1, k] * masked[k]
                along = swim * (coef[3, k] * masked[k])
                across = swim * (coef[2, k] * masked[k])
                sides = east(plain + across) + west(plain - across)
                ends = within(plain + along, 7) + within(plain - along, 1)
                pulled[c, k] = fields[0, k] * (coef[0, k] * masked[k] + (ends + sides))

    return begin, each, nothing


def pull_halo_kernel(age, speed, fields, halo_fields, before, after, rims, both_out, coef, own, edge):
    def begin():
        transport_coef(halo_fields, coef)
        row = rows_of(own.shape[1:])
        side = rim(fields[2, 0], fields[2, 1])
        own[0] = rim(fields[3, 0], fields[3, 1])
        own[1] = jnp.where(row < 4, side, -side)
        own[2] = rim(fields[0, 0], fields[0, 1])

    def each(group):
        for slot, c in enumerate(group):
            join(before[c], after[c], edge.at[slot])
        for slot, c in enumerate(group):
            swim = speed[age[c]]
            masked = halo_fields[0] * edge[slot]
            plain = coef[1] * masked
            along = swim * (coef[3] * masked)
            across = swim * (coef[2] * masked)
            onward, backward = plain + along, plain - along
            sides = east(plain + across) + west(plain - across)
            north, south = halo_neighbours((own[0] + swim * own[1]) * rims[c], onward, backward)
            grad = coef[0] * masked + ((north + south) + sides)
            more = jnp.where(rows_of(grad.shape) < 4, backward, onward)
            both_out[c] = combine(halo_fields[0] * grad, own[2] * more)

    return begin, each, nothing


def whole_tiles(tiles, both, c):
    more = addends(both[c])
    return [tiles[c, 0] + more[0], tiles[c, 1] + more[1], both[c]]


def backward_kernel(age, mort, crowding, speed, fields, halo_fields, crowd, crowd_two, sums, pulled, pulled_both, state,
                    state_both, start, partial, totals, coef):
    pressure, later = totals.at[0:3], totals.at[3:5]

    def begin():
        for k in range(4):
            totals[5 + k] = sums[2 + k // 2, k % 2]
        for k in range(3):
            field = lambda n: fields[n, k] if k < 2 else halo_fields[n]
            coef[0, k] = 1.0 - 4.0 * field(3)
            coef[1, k] = field(3)
            coef[2, k] = field(1)
            coef[3, k] = field(2)
        clear(pressure, later)

    def each(group):
        for c in group:
            mortal, crowded, swim = [table[age[c]] for table in (mort, crowding, speed)]
            grad, now = whole_tiles(pulled, pulled_both, c), whole_tiles(state, state_both, c)
            value = []
            for k in range(3):
                value.append(grad[k] * decays(mortal, crowded, crowd_two[k]))
                pressure[k] -= crowded * (value[k] * now[k])
            plain = [coef[1, k] * value[k] for k in range(3)]
            along = [swim * (coef[3, k] * value[k]) for k in range(3)]
            north = northern(*[plain[k] + along[k] for k in range(3)])
            south = southern(*[plain[k] - along[k] for k in range(3)])
            for k in range(2):
                across = swim * (coef[2, k] * value[k])
                sides = east(plain[k] + across) + west(plain[k] - across)
                spread = coef[0, k] * value[k] + ((north[k] + south[k]) + sides)
                mine = (fields[0, k] * decays(mortal, crowded, crowd[k])) * spread
                partial[c, k] = mine
                later[k] -= crowded * (start[c, k] * mine)

    return begin, each, nothing


def shares_kernel(age, mort, crowding, speed, fields, crowd, crowd_two, sums, halo_sums, cotangent, pulled, pulled_both, start,
                  wet_halo, state, state_both, shares):
    def begin():
        clear(shares)
        plain, swum = [[sums[n, 0], sums[n, 1], halo_sums[n]] for n in range(2)]
        plain_north, plain_south = northern(*plain), southern(*plain)
        swum_north, swum_south = northern(*swum), southern(*swum)
        for k in range(2):
            ocean = fields[0, k]
            shares[3, k] = (-0.5 * ocean) * (east(swum[k]) - west(swum[k]))
            shares[4, k] = (-0.5 * ocean) * (swum_north[k] - swum_south[k])
            around = plain_north[k] + plain_south[k] + east(plain[k]) + west(plain[k])
            shares[5, k] = ocean * (around - 4.0 * plain[k])

    def each(group):
        for c in group:
            mortal, crowded, swim = [table[age[c]] for table in (mort, crowding, speed)]
            old = [start[c, k] * (fields[0, k] * decays(mortal, crowded, crowd[k])) for k in range(2)] + [wet_halo[c]]
            fade = [decays(mortal, crowded, crowd_two[k]) for k in range(3)]
            new = [tile * fade[k] for k, tile in enumerate(whole_tiles(state, state_both, c))]
            grad = whole_tiles(pulled, pulled_both, c)
            for wet, weigh in ((old, lambda k: grad[k] * fade[k]), (new, lambda k: fields[0, k] * cotangent[c, k])):
                north, south = northern(*wet), southern(*wet)
                for k in range(2):
                    by = weigh(k)
                    to_east, to_west = east(wet[k]), west(wet[k])
                    pace = (-0.5 * swim) * by
                    shares[0, k] += pace * (to_east - to_west)
                    shares[1, k] += pace * (north[k] - south[k])
                    shares[2, k] += by * ((north[k] + south[k]) + (to_east + to_west) - 4.0 * wet[k])

    return begin, each, nothing


def last_kernel(age, mort, crowding, mass, speed, totals, fields, halo_fields, crowd, partial, out, terms):
    pressure = totals.at[0:3]

    def begin():
        field = lambda n, k: fields[n, k] if k < 2 else halo_fields[n]
        value = [field(0, k) * (pressure[k] * (1.0 / COH)) for k in range(3)]
        plain = [field(3, k) * value[k] for k in range(3)]
        along = [field(2, k) * value[k] for k in range(3)]
        north, south = northern(*plain), southern(*plain)
        drift_north, drift_south = northern(*along), southern(*along)
        for k in range(2):
            across = fields[1, k] * value[k]
            still = (1.0 - 4.0 * fields[3, k]) * value[k]
            still += (north[k] + south[k]) + (east(plain[k]) + west(plain[k]))
            moving = (drift_north[k] - drift_south[k]) + (east(across) - west(across))
            terms[0, k] = fields[0, k] * still
            terms[1, k] = fields[0, k] * moving
            terms[2, k] = (totals[3 + k] - totals[5 + k] * still - totals[7 + k] * moving) * (1.0 / COH)

    def each(group):
        for c in group:
            mortal, crowded, weight, swim = [table[age[c]] for table in (mort, crowding, mass, speed)]
            for k in range(2):
                term = decays(mortal, crowded, crowd[k]) * (terms[0, k] + swim * terms[1, k]) + terms[2, k]
                out[c, k] = partial[c, k] + weight * term

    return begin, each, nothing


def driver(kernel, cohorts, sides, n_small, n_in, n_out, n_whole, n_scratch, *refs):
    refs = list(refs)

    def take(count):
        taken, refs[:] = refs[:count], refs[count:]
        return taken

    small, sources, sinks, wholes, scratch = take(n_small), take(n_in), take(n_out), take(n_whole), take(n_scratch)
    inside, outside = take(n_in), take(n_out)
    groups = cohorts // STEP

    def span(group):
        return pl.ds(pl.multiple_of(group * STEP, STEP) if not isinstance(group, int) else group * STEP, STEP)

    def loads(group):
        return [pltpu.make_async_copy(a.at[span(group)], b.at[span(group)], refs[0].at[n, group])
                for n, (a, b) in enumerate(zip(sources, inside))]

    def stores(group):
        return [pltpu.make_async_copy(b.at[span(group)], a.at[span(group)], refs[-1].at[n, group])
                for n, (a, b) in enumerate(zip(sinks, outside))]

    for group in range(groups):
        for copy in loads(group):
            copy.start()

    def run(arrays):
        begin, each, end = kernel(*arrays)
        begin()

        def step(group, _):
            for copy in loads(group):
                copy.wait()
            each([group * STEP + slot for slot in range(STEP)])
            for copy in stores(group):
                copy.start()
            return 0

        lax.fori_loop(0, groups, step, 0)
        end()

    arrays = small + inside + outside + wholes + scratch
    if sides is None:
        run(arrays)
    else:
        even, arrays = arrays[0], arrays[1:]
        turned = list(arrays)
        turned[sides], turned[sides + 1] = arrays[sides + 1], arrays[sides]

        @pl.when(even[0] == 1)
        def _():
            run(turned if sides < n_small else arrays)

        @pl.when(even[0] == 0)
        def _():
            run(arrays if sides < n_small else turned)

    for group in range(groups):
        for copy in stores(group):
            copy.wait()


SMEM = pl.BlockSpec(memory_space=pltpu.SMEM)
VMEM = pl.BlockSpec(memory_space=pltpu.VMEM)
LARGE = pl.BlockSpec(memory_space=pl.ANY)


def call(kernel, tables, small, large, large_outs, outs, scratch, cycles, sides=None):
    cohorts = large[0].shape[0]
    groups = cohorts // STEP
    vmem = lambda shape: pltpu.VMEM(shape, F32)
    sems = [pltpu.SemaphoreType.DMA((len(arrays), groups)) for arrays in (large, large_outs) if arrays]
    outputs = pl.pallas_call(
        functools.partial(driver, kernel, cohorts, sides, len(tables) + len(small), len(large), len(large_outs), len(outs), len(scratch)),
        in_specs=[SMEM] * len(tables) + [VMEM] * len(small) + [LARGE] * len(large),
        out_specs=[LARGE] * len(large_outs) + [VMEM] * len(outs),
        out_shape=[pltpu.HBM(shape, F32) for shape in large_outs] + [jax.ShapeDtypeStruct(shape, F32) for shape in outs],
        scratch_shapes=[vmem(shape) for shape in scratch] + [vmem(x.shape) for x in large]
        + [vmem(shape) for shape in large_outs] + sems,
        compiler_params=pltpu.CompilerParams(vmem_limit_bytes=32 << 20),
        cost_estimate=pl.CostEstimate(flops=cycles, transcendentals=0, bytes_accessed=cycles),
    )(*tables, *small, *[stay(x) for x in large])
    count = len(large_outs)
    return [stay(x) for x in outputs[:count]] + list(outputs[count:])


def swap(value, flip):
    return lax.ppermute(value, "coh", [(i, i ^ flip) for i in range(4)])


def total_of(value):
    value = value + swap(value, 1)
    return value + swap(value, 2)


def halves(value, side):
    middle = value.shape[-1] // 2
    low, high = value[..., :middle], value[..., middle:]
    return jnp.where(side == 0, low, high), jnp.where(side == 0, high, low)


def total_by_halves(value):
    side = lax.axis_index("coh") % 2
    keep, send = halves(value, side)
    keep = keep + swap(send, 1)
    keep = keep + swap(keep, 2)
    other = swap(keep, 1)
    return jnp.where(side == 0, jnp.concatenate([keep, other], -1), jnp.concatenate([other, keep], -1))


def quarter(value):
    side, block = lax.axis_index("coh") % 2, lax.axis_index("coh") // 2
    fourth = value.shape[-1] // 4
    parts = [value[..., k * fourth : (k + 1) * fourth] for k in range(4)]
    keep = [jnp.where(side == 0, parts[2 * k], parts[2 * k + 1]) for k in range(2)]
    send = [jnp.where(side == 0, parts[2 * k + 1], parts[2 * k]) for k in range(2)]
    return keep, send, block


def scatter(value):
    keep, send, block = quarter(value)
    got = swap(jnp.stack(send), 1)
    keep = [keep[0] + got[0], keep[1] + got[1]]
    mine = jnp.where(block == 0, keep[0], keep[1])
    rest = jnp.where(block == 0, keep[1], keep[0])
    return mine + swap(rest, 2)


def near_swap(value, count):
    return lax.ppermute(value, "lat", [(i, i ^ 1) for i in range(count)])


def far_swap(value, count):
    return lax.ppermute(value, "lat", [(i, ((i + 1) ^ 1) - 1) for i in range(1, count - 1)])


def local(density, cotangent, land_mask, east_vel, north_vel, diffusion, age_class, mort_rate, crowd_coef, mass, speed):
    age_class, mort_rate, crowd_coef, mass, speed = [stay(x) for x in (age_class, mort_rate, crowd_coef, mass, speed)]
    raw_fields = [stay(x) for x in (land_mask, east_vel, north_vel, diffusion)]
    count = lax.axis_size("lat")
    odd = lax.axis_index("lat") % 2
    even = (1 - odd).astype(jnp.int32)[None]
    cohorts, _, height, lon = density.shape
    main, halo, edge = (cohorts, 2, height, lon), (cohorts, height, lon), (cohorts, 4, lon)
    tiles, three, fields_shape = (2, height, lon), (3, height, lon), (4, 3, height, lon)

    wide = (cohorts + 5, 4, lon)
    (crowd,) = call(crowd_kernel, [age_class, mass], [], [density], [], [tiles], [], 2000)
    crowd = total_of(crowd)
    near, far = call(edges_kernel, [even], raw_fields, [density], [], [wide, wide], [], 2000, sides=len(raw_fields) + 1)
    late_near, late_far = call(edges_kernel, [even], [], [cotangent], [], [edge, edge], [], 2000, sides=1)

    def edge_rows(value, start):
        return value[:, start : start + 2].reshape(4, lon)

    up, down = edge_rows(crowd, height - 2), edge_rows(crowd, 0)
    far = far.at[cohorts + 4].set(jnp.where(odd == 1, up, down))
    near = near.at[cohorts + 4].set(jnp.where(odd == 1, down, up))
    far = far_swap(far, count)
    near = near_swap(near, count)
    late_far = far_swap(late_far, count)
    late_near = near_swap(late_near, count)

    tables = [age_class, mort_rate, crowd_coef, mass, speed]
    own_fields, halo_fields_shape = (4,) + tiles, (4, height, lon)
    state, rims, fields, crowd_two, sums = call(
        forward_kernel, tables, raw_fields + [crowd], [density],
        [main, halo], [own_fields, tiles, (4,) + tiles], [own_fields], 4000)
    pulled, late_rims = call(
        pull_kernel, [age_class, speed], [fields], [cotangent], [main, halo], [], [own_fields], 4000)
    state_both, wet_halo, halo_fields, crowd_two, halo_sums = call(
        forward_halo_kernel, [even] + tables, [fields, crowd_two, near, far], [rims],
        [halo, halo], [halo_fields_shape, three, (2, height, lon)],
        [halo_fields_shape, (2, height, lon), (height, lon), (STEP, height, lon), (height, lon)], 2500, sides=7)
    crowd_two = total_of(crowd_two)
    (pulled_both,) = call(
        pull_halo_kernel, [even, age_class, speed], [fields, halo_fields, late_near, late_far], [late_rims],
        [halo], [], [halo_fields_shape, (3, height, lon), (STEP, height, lon)], 2500, sides=4)

    tables = [age_class, mort_rate, crowd_coef, speed]
    partial, totals = call(
        backward_kernel, tables, [fields, halo_fields, crowd, crowd_two, sums],
        [pulled, pulled_both, state, state_both, density], [main], [(9, height, lon)], [fields_shape], 5000)
    totals = total_by_halves(totals)

    (shares,) = call(
        shares_kernel, tables, [fields, crowd, crowd_two, sums, halo_sums],
        [cotangent, pulled, pulled_both, density, wet_halo, state, state_both], [], [(6,) + tiles], [], 6000)
    shares = scatter(shares)

    (grad,) = call(
        last_kernel, [age_class, mort_rate, crowd_coef, mass, speed],
        [totals, fields, halo_fields, crowd], [partial], [main], [], [(3,) + tiles], 3000)

    fourth = lon // 4
    mine = lax.dynamic_slice_in_dim(totals[:2], lax.axis_index("coh") * fourth, fourth, axis=2)
    shares = shares[:3] + shares[3:] * (mine * (1.0 / COH))[None]
    return (grad, shares[0], shares[1], shares[2])


def solution(mesh):
    spread_spec = P("coh", None, "lat", None)
    field_spec = P(None, "lat", None)
    in_specs = (spread_spec, spread_spec) + (field_spec,) * 4 + (P("coh"),) + (P(),) * 4
    out_specs = (spread_spec,) + (P(None, "lat", "coh"),) * 3
    return jax.shard_map(local, mesh=mesh, in_specs=in_specs, out_specs=out_specs, check_vma=False)
```

```python
import functools

import jax
import jax.numpy as jnp
from jax import lax
from jax.experimental import pallas as pl
from jax.experimental.pallas import tpu as pltpu
from jax.sharding import PartitionSpec as P


COH = 128
LOG2E = 1.4426950408889634
STEP = 8
LAND = 1e7
F32 = jnp.float32


def rows_of(shape):
    return lax.broadcasted_iota(jnp.int32, shape, 0)


def turn(tile, shift):
    return pltpu.roll(tile, shift, 0)


def east(tile):
    return pltpu.roll(tile, tile.shape[1] - 1, 1)


def west(tile):
    return pltpu.roll(tile, 1, 1)


def northern(first, second, halo):
    row = rows_of(first.shape)
    return (
        jnp.where(row == 7, turn(halo, 3), turn(first, 7)),
        jnp.where(row == 7, turn(halo, 1), turn(second, 7)),
    )


def southern(first, second, halo):
    row = rows_of(first.shape)
    return (
        jnp.where(row == 0, turn(halo, 7), turn(first, 1)),
        jnp.where(row == 0, turn(halo, 5), turn(second, 1)),
    )


def within(tile, shift):
    return jnp.where(rows_of(tile.shape) == (0 if shift == 1 else 7), 0.0, turn(tile, shift))


def rim(first, second):
    row = rows_of(first.shape)
    last = jnp.where(row == 4, turn(first, 5), turn(second, 7))
    return jnp.where(row == 1, turn(first, 1), jnp.where(row == 3, turn(second, 3), last))


def halo_neighbours(own, north, south):
    row = rows_of(own.shape)
    lower, upper = (row == 1) | (row == 3), (row == 4) | (row == 6)
    return jnp.where(lower, own, turn(north, 7)), jnp.where(upper, own, turn(south, 1))


def combine(inner, added):
    row = rows_of(inner.shape)
    used = (row == 1) | (row == 3) | (row == 4) | (row == 6)
    return jnp.where(used, inner, jnp.where(row < 4, turn(added, 7), turn(added, 1)))


def addends(both):
    row = rows_of(both.shape)
    return (
        jnp.where(row == 0, both, jnp.where(row == 7, turn(both, 2), 0.0)),
        jnp.where(row == 7, both, jnp.where(row == 0, turn(both, 6), 0.0)),
    )


def stay(value):
    return pltpu.with_memory_space_constraint(value, pltpu.HBM)


def decays(mortal, crowded, crowd):
    return jnp.exp2(-LOG2E * mortal - (LOG2E / COH * crowded) * crowd)


def join(before, after, out):
    out[0:4, :] = before
    out[4:8, :] = after


def pack(source, up, down, slot):
    for out, start in ((up, 6), (down, 0)):
        out[slot, 0:2, :] = source(0, start)
        out[slot, 2:4, :] = source(1, start)


def clear(*refs):
    for ref in refs:
        ref[...] = jnp.zeros_like(ref)


def nothing():
    pass


def first_kernel(age, mass, ocean, east_vel, north_vel, kappa, state, up, down, crowd):
    cohorts = state.shape[0]

    def begin():
        clear(crowd)

    def each(group):
        for layer in range(2):
            crowd[layer] += sum(mass[age[c]] * state[c, layer] for c in group)
        for c in group:
            pack(lambda layer, start: state[c, layer, start : start + 2, :], up, down, c)

    def end():
        for slot, field in enumerate((ocean, east_vel, north_vel, kappa)):
            pack(lambda layer, start: field[layer, start : start + 2, :].astype(F32), up, down, cohorts + slot)

    return begin, each, end


def edges_kernel(state, up, down):
    def each(group):
        for c in group:
            pack(lambda layer, start: state[c, layer, start : start + 2, :], up, down, c)

    return nothing, each, nothing


def forward_kernel(age, mort, crowding, mass, speed, ocean, east_vel, north_vel, kappa, crowd, state,
                   state_out, rims, fields, crowd_out, total, sums, coef):
    def begin():
        clear(total, sums)
        for slot, (field, scale) in enumerate(((ocean, None), (east_vel, 0.5), (north_vel, 0.5), (kappa, None))):
            for layer in range(2):
                fields[slot, layer] = field[layer].astype(F32)
            if scale is not None:
                fields[slot] = scale * fields[slot]
        coef[0] = fields[0] * (1.0 - 4.0 * fields[3])
        coef[1] = fields[0] * fields[3]
        coef[2] = fields[0] * fields[1]
        coef[3] = fields[0] * fields[2]
        crowd_out[...] = jnp.where(fields[0] == 0.0, LAND, crowd[...])

    def each(group):
        for c in group:
            mortal, crowded, weight, swim = [table[age[c]] for table in (mort, crowding, mass, speed)]
            wet = [state[c, k] * decays(mortal, crowded, crowd_out[k]) for k in range(2)]
            rims[c] = rim(*wet)
            for k in range(2):
                north, south, to_east, to_west = within(wet[k], 7), within(wet[k], 1), east(wet[k]), west(wet[k])
                around = (north + south) + (to_east + to_west)
                drift = coef[2, k] * (to_east - to_west) + coef[3, k] * (north - south)
                moved = coef[0, k] * wet[k] + coef[1, k] * around - swim * drift
                state_out[c, k] = moved
                total[k] += weight * moved
                mine = weight * wet[k]
                swum = swim * mine
                sums[0, k] += mine
                sums[1, k] += swum
                sums[2, k] += crowded * mine
                sums[3, k] += crowded * swum

    return begin, each, nothing


def forward_halo_kernel(age, mort, crowding, mass, speed, fields, total, before, after, crowd_before, crowd_after, rims,
                        both_out, wet_out, halo_fields, total_out, sums, coef, own, crowd, edge, added):
    def begin():
        clear(sums, added)
        cohorts = rims.shape[0]
        for slot, scale in enumerate((None, 0.5, 0.5, None)):
            join(before[cohorts + slot], after[cohorts + slot], edge.at[0])
            halo_fields[slot] = edge[0] if scale is None else scale * edge[0]
        ocean = halo_fields[0]
        coef[0] = ocean * (1.0 - 4.0 * halo_fields[3])
        coef[1] = ocean * halo_fields[3]
        coef[2] = ocean * halo_fields[1]
        coef[3] = ocean * halo_fields[2]
        row = rows_of(ocean.shape)
        ocean = rim(fields[0, 0], fields[0, 1])
        own[0] = ocean * rim(fields[3, 0], fields[3, 1])
        own[1] = jnp.where(row < 4, ocean, -ocean) * rim(fields[2, 0], fields[2, 1])
        join(crowd_before[...], crowd_after[...], crowd)
        crowd[...] = jnp.where(halo_fields[0] == 0.0, LAND, crowd[...])

    def each(group):
        for slot, c in enumerate(group):
            join(before[c], after[c], edge.at[slot])
        for slot, c in enumerate(group):
            mortal, crowded, weight, swim = [table[age[c]] for table in (mort, crowding, mass, speed)]
            wet = edge[slot] * decays(mortal, crowded, crowd[...])
            wet_out[c] = wet
            north, south = halo_neighbours(rims[c], wet, wet)
            to_east, to_west = east(wet), west(wet)
            around = (north + south) + (to_east + to_west)
            drift = coef[2] * (to_east - to_west) + coef[3] * (north - south)
            moved = coef[0] * wet + coef[1] * around - swim * drift
            both = combine(moved, (own[0] + swim * own[1]) * wet)
            both_out[c] = both
            added[...] += weight * both
            mine = weight * wet
            sums[0] += mine
            sums[1] += swim * mine

    def end():
        total_out[2] = added[...]
        for k, more in enumerate(addends(added[...])):
            total_out[k] = total[k] + more

    return begin, each, end


def transport_coef(fields, coef):
    coef[0] = 1.0 - 4.0 * fields[3]
    coef[1] = fields[3]
    coef[2] = fields[1]
    coef[3] = fields[2]


def pull_kernel(age, speed, fields, cotangent, pulled, rims, coef):
    def begin():
        transport_coef(fields, coef)

    def each(group):
        for c in group:
            swim = speed[age[c]]
            masked = [fields[0, k] * cotangent[c, k] for k in range(2)]
            rims[c] = rim(*masked)
            for k in range(2):
                plain = coef[1, k] * masked[k]
                along = swim * (coef[3, k] * masked[k])
                across = swim * (coef[2, k] * masked[k])
                sides = east(plain + across) + west(plain - across)
                ends = within(plain + along, 7) + within(plain - along, 1)
                pulled[c, k] = fields[0, k] * (coef[0, k] * masked[k] + (ends + sides))

    return begin, each, nothing


def pull_halo_kernel(age, speed, fields, halo_fields, before, after, rims, both_out, coef, own, edge):
    def begin():
        transport_coef(halo_fields, coef)
        row = rows_of(own.shape[1:])
        side = rim(fields[2, 0], fields[2, 1])
        own[0] = rim(fields[3, 0], fields[3, 1])
        own[1] = jnp.where(row < 4, side, -side)
        own[2] = rim(fields[0, 0], fields[0, 1])

    def each(group):
        for slot, c in enumerate(group):
            join(before[c], after[c], edge.at[slot])
        for slot, c in enumerate(group):
            swim = speed[age[c]]
            masked = halo_fields[0] * edge[slot]
            plain = coef[1] * masked
            along = swim * (coef[3] * masked)
            across = swim * (coef[2] * masked)
            onward, backward = plain + along, plain - along
            sides = east(plain + across) + west(plain - across)
            north, south = halo_neighbours((own[0] + swim * own[1]) * rims[c], onward, backward)
            grad = coef[0] * masked + ((north + south) + sides)
            more = jnp.where(rows_of(grad.shape) < 4, backward, onward)
            both_out[c] = combine(halo_fields[0] * grad, own[2] * more)

    return begin, each, nothing


def whole_tiles(tiles, both, c):
    more = addends(both[c])
    return [tiles[c, 0] + more[0], tiles[c, 1] + more[1], both[c]]


def backward_kernel(age, mort, crowding, speed, fields, halo_fields, crowd, crowd_two, sums, pulled, pulled_both, state,
                    state_both, start, partial, totals, coef):
    pressure, later = totals.at[0:3], totals.at[3:5]

    def begin():
        for k in range(4):
            totals[5 + k] = sums[2 + k // 2, k % 2]
        for k in range(3):
            field = lambda n: fields[n, k] if k < 2 else halo_fields[n]
            coef[0, k] = 1.0 - 4.0 * field(3)
            coef[1, k] = field(3)
            coef[2, k] = field(1)
            coef[3, k] = field(2)
        clear(pressure, later)

    def each(group):
        for c in group:
            mortal, crowded, swim = [table[age[c]] for table in (mort, crowding, speed)]
            grad, now = whole_tiles(pulled, pulled_both, c), whole_tiles(state, state_both, c)
            value = []
            for k in range(3):
                value.append(grad[k] * decays(mortal, crowded, crowd_two[k]))
                pressure[k] -= crowded * (value[k] * now[k])
            plain = [coef[1, k] * value[k] for k in range(3)]
            along = [swim * (coef[3, k] * value[k]) for k in range(3)]
            north = northern(*[plain[k] + along[k] for k in range(3)])
            south = southern(*[plain[k] - along[k] for k in range(3)])
            for k in range(2):
                across = swim * (coef[2, k] * value[k])
                sides = east(plain[k] + across) + west(plain[k] - across)
                spread = coef[0, k] * value[k] + ((north[k] + south[k]) + sides)
                mine = decays(mortal, crowded, crowd[k]) * spread
                partial[c, k] = mine
                later[k] -= crowded * (start[c, k] * mine)

    return begin, each, nothing


def shares_kernel(age, mort, crowding, speed, fields, crowd, crowd_two, sums, halo_sums, pulled, pulled_both, wet_halo, state,
                  state_both, cotangent, start, shares):
    def begin():
        clear(shares)
        plain, swum = [[sums[n, 0], sums[n, 1], halo_sums[n]] for n in range(2)]
        plain_north, plain_south = northern(*plain), southern(*plain)
        swum_north, swum_south = northern(*swum), southern(*swum)
        for k in range(2):
            ocean = fields[0, k]
            shares[3, k] = (-0.5 * ocean) * (east(swum[k]) - west(swum[k]))
            shares[4, k] = (-0.5 * ocean) * (swum_north[k] - swum_south[k])
            around = plain_north[k] + plain_south[k] + east(plain[k]) + west(plain[k])
            shares[5, k] = ocean * (around - 4.0 * plain[k])

    def each(group):
        for c in group:
            mortal, crowded, swim = [table[age[c]] for table in (mort, crowding, speed)]
            old = [start[c, k] * decays(mortal, crowded, crowd[k]) for k in range(2)] + [wet_halo[c]]
            fade = [decays(mortal, crowded, crowd_two[k]) for k in range(3)]
            new = [tile * fade[k] for k, tile in enumerate(whole_tiles(state, state_both, c))]
            grad = whole_tiles(pulled, pulled_both, c)
            for wet, weigh in ((old, lambda k: grad[k] * fade[k]), (new, lambda k: fields[0, k] * cotangent[c, k])):
                north, south = northern(*wet), southern(*wet)
                for k in range(2):
                    by = weigh(k)
                    to_east, to_west = east(wet[k]), west(wet[k])
                    pace = (-0.5 * swim) * by
                    shares[0, k] += pace * (to_east - to_west)
                    shares[1, k] += pace * (north[k] - south[k])
                    shares[2, k] += by * ((north[k] + south[k]) + (to_east + to_west) - 4.0 * wet[k])

    return begin, each, nothing


def last_kernel(age, mort, crowding, mass, speed, totals, fields, halo_fields, crowd, partial, out, terms):
    pressure = totals.at[0:3]

    def begin():
        field = lambda n, k: fields[n, k] if k < 2 else halo_fields[n]
        value = [field(0, k) * (pressure[k] * (1.0 / COH)) for k in range(3)]
        plain = [field(3, k) * value[k] for k in range(3)]
        along = [field(2, k) * value[k] for k in range(3)]
        north, south = northern(*plain), southern(*plain)
        drift_north, drift_south = northern(*along), southern(*along)
        for k in range(2):
            across = fields[1, k] * value[k]
            still = (1.0 - 4.0 * fields[3, k]) * value[k]
            still += (north[k] + south[k]) + (east(plain[k]) + west(plain[k]))
            moving = (drift_north[k] - drift_south[k]) + (east(across) - west(across))
            terms[0, k] = still
            terms[1, k] = moving
            terms[2, k] = (totals[3 + k] - totals[5 + k] * still - totals[7 + k] * moving) * (1.0 / COH)

    def each(group):
        for c in group:
            mortal, crowded, weight, swim = [table[age[c]] for table in (mort, crowding, mass, speed)]
            for k in range(2):
                term = decays(mortal, crowded, crowd[k]) * (terms[0, k] + swim * terms[1, k]) + terms[2, k]
                out[c, k] = partial[c, k] + weight * term

    return begin, each, nothing


def driver(kernel, cohorts, sides, n_tables, n_small, n_in, n_out, n_whole, n_scratch, *refs):
    refs = list(refs)

    def take(count):
        taken, refs[:] = refs[:count], refs[count:]
        return taken

    tables = take(n_tables)
    small, sources, sinks, wholes, scratch = take(n_small), take(n_in), take(n_out), take(n_whole), take(n_scratch)
    inside, outside, held = take(n_in), take(n_out), take(n_tables)
    table_sem = refs.pop()
    lookups = [pltpu.make_async_copy(a, b, table_sem.at[n]) for n, (a, b) in enumerate(zip(tables, held))]
    for copy in lookups:
        copy.start()
    groups = cohorts // STEP

    def span(group):
        return pl.ds(pl.multiple_of(group * STEP, STEP) if not isinstance(group, int) else group * STEP, STEP)

    def loads(group):
        return [pltpu.make_async_copy(a.at[span(group)], b.at[span(group)], refs[0].at[n, group])
                for n, (a, b) in enumerate(zip(sources, inside))]

    def stores(group):
        return [pltpu.make_async_copy(b.at[span(group)], a.at[span(group)], refs[-1].at[n, group])
                for n, (a, b) in enumerate(zip(sinks, outside))]

    for group in range(groups):
        for copy in loads(group):
            copy.start()

    for copy in lookups:
        copy.wait()

    def run(arrays):
        begin, each, end = kernel(*arrays)
        begin()

        def step(group, _):
            for copy in loads(group):
                copy.wait()
            each([group * STEP + slot for slot in range(STEP)])
            for copy in stores(group):
                copy.start()
            return 0

        lax.fori_loop(0, groups, step, 0)
        end()

    arrays = held + small + inside + outside + wholes + scratch
    n_small += n_tables
    if sides is None:
        run(arrays)
    else:
        even, arrays = arrays[0], arrays[1:]
        turned = list(arrays)
        for side in sides:
            turned[side], turned[side + 1] = arrays[side + 1], arrays[side]

        @pl.when(even[0] == 1)
        def _():
            run(turned if sides[0] < n_small else arrays)

        @pl.when(even[0] == 0)
        def _():
            run(arrays if sides[0] < n_small else turned)

    for group in range(groups):
        for copy in stores(group):
            copy.wait()


VMEM_BYTES = {"first": 8, "late_edges": 6, "forward": 8, "pull": 8, "forward_halo": 8, "pull_halo": 8, "backward": 8,
              "shares": 10, "last": 8}
VMEM = pl.BlockSpec(memory_space=pltpu.VMEM)
LARGE = pl.BlockSpec(memory_space=pl.ANY)


def call(name, kernel, cohorts, tables, small, large, large_outs, outs, scratch, cycles, sides=None):
    groups = cohorts // STEP
    vmem = lambda shape: pltpu.VMEM(shape, F32)
    sems = [pltpu.SemaphoreType.DMA((len(arrays), groups)) for arrays in (large, large_outs) if arrays]
    outputs = pl.pallas_call(
        functools.partial(driver, kernel, cohorts, sides, len(tables), len(small), len(large), len(large_outs), len(outs), len(scratch)),
        in_specs=[LARGE] * len(tables) + [VMEM] * len(small) + [LARGE] * len(large),
        out_specs=[LARGE] * len(large_outs) + [VMEM] * len(outs),
        out_shape=[pltpu.HBM(shape, F32) for shape in large_outs] + [jax.ShapeDtypeStruct(shape, F32) for shape in outs],
        scratch_shapes=[vmem(shape) for shape in scratch] + [vmem(x.shape) for x in large]
        + [vmem(shape) for shape in large_outs] + [(pltpu.SMEM if x.ndim == 1 else pltpu.VMEM)(x.shape, x.dtype) for x in tables]
        + sems + [pltpu.SemaphoreType.DMA((len(tables),))],
        compiler_params=pltpu.CompilerParams(vmem_limit_bytes=VMEM_BYTES[name] << 20),
        cost_estimate=pl.CostEstimate(flops=cycles, transcendentals=0, bytes_accessed=cycles),
    )(*[stay(x) for x in tables], *small, *[stay(x) for x in large])
    count = len(large_outs)
    return [stay(x) for x in outputs[:count]] + list(outputs[count:])


def swap(value, flip):
    return lax.ppermute(value, "coh", [(i, i ^ flip) for i in range(4)])


def total_of(value):
    value = value + swap(value, 1)
    return value + swap(value, 2)


def total_by_halves(value, lower):
    middle = value.shape[-1] // 2
    low, high = value[..., :middle], value[..., middle:]
    keep, send = jnp.where(lower, low, high), jnp.where(lower, high, low)
    keep = keep + swap(send, 1)
    keep = keep + swap(keep, 2)
    other = swap(keep, 1)
    return jnp.where(lower, jnp.concatenate([keep, other], -1), jnp.concatenate([other, keep], -1))


def scatter(value, lower, first):
    fourth = value.shape[-1] // 4
    parts = [value[..., k * fourth : (k + 1) * fourth] for k in range(4)]
    keep = [jnp.where(lower, parts[2 * k], parts[2 * k + 1]) for k in range(2)]
    send = [jnp.where(lower, parts[2 * k + 1], parts[2 * k]) for k in range(2)]
    got = swap(jnp.stack(send), 1)
    keep = [keep[0] + got[0], keep[1] + got[1]]
    mine, rest = jnp.where(first, keep[0], keep[1]), jnp.where(first, keep[1], keep[0])
    return mine + swap(rest, 2)


def near_swap(value, count):
    return lax.ppermute(value, "lat", [(i, i ^ 1) for i in range(count)])


def far_swap(value, count):
    return lax.ppermute(value, "lat", [(i, ((i + 1) ^ 1) - 1) for i in range(1, count - 1)])


def local(density, cotangent, land_mask, east_vel, north_vel, diffusion, age_class, mort_rate, crowd_coef, mass, speed):
    age_class, mort_rate, crowd_coef, mass, speed = [stay(x) for x in (age_class, mort_rate, crowd_coef, mass, speed)]
    raw_fields = [stay(x) for x in (land_mask, east_vel, north_vel, diffusion)]
    count = lax.axis_size("lat")
    strip, group = lax.axis_index("lat") & 1, lax.axis_index("coh")
    choices = (1 - strip).astype(jnp.int32)[None], strip == 1, (group & 1) == 0, (group & 2) == 0
    density, (even, odd, lower, first) = lax.optimization_barrier((density, choices))
    cohorts, _, height, lon = density.shape
    main, halo, edge = (cohorts, 2, height, lon), (cohorts, height, lon), (cohorts, 4, lon)
    tiles, three, fields_shape = (2, height, lon), (3, height, lon), (4, 3, height, lon)

    wide = (cohorts + 4, 4, lon)
    near, far, crowd = call("first", first_kernel, cohorts, [even, age_class, mass] + raw_fields, [], [density], [], [wide, wide, tiles], [],
                            2000, sides=(len(raw_fields) + 3,))
    crowd = total_of(crowd)
    late_near, late_far = call("late_edges", edges_kernel, cohorts, [even], [], [cotangent], [], [edge, edge], [], 2000, sides=(1,))

    def edge_rows(value, start):
        return value[:, start : start + 2].reshape(4, lon)

    up, down = edge_rows(crowd, height - 2), edge_rows(crowd, 0)
    crowd_far = far_swap(jnp.where(odd, up, down), count)
    crowd_near = near_swap(jnp.where(odd, down, up), count)
    far = far_swap(far, count)
    near = near_swap(near, count)
    late_far = far_swap(late_far, count)
    late_near = near_swap(late_near, count)

    tables = [age_class, mort_rate, crowd_coef, mass, speed]
    own_fields, halo_fields_shape = (4,) + tiles, (4, height, lon)
    state, rims, fields, crowd, crowd_two, sums = call("forward", forward_kernel, cohorts, tables + raw_fields, [crowd], [density],
        [], [main, halo, own_fields, tiles, tiles, (4,) + tiles], [own_fields], 4000)
    pulled, late_rims = call("pull", pull_kernel, cohorts, [age_class, speed], [fields], [cotangent], [], [main, halo], [own_fields], 4000)
    state_both, wet_halo, halo_fields, crowd_two, halo_sums = call("forward_halo", forward_halo_kernel, cohorts, [even] + tables, [fields, crowd_two, near, far, crowd_near, crowd_far, rims], [],
        [], [halo, halo, halo_fields_shape, three, (2, height, lon)],
        [halo_fields_shape, (2, height, lon), (height, lon), (STEP, height, lon), (height, lon)], 2500, sides=(7, 9))
    crowd_two = total_of(crowd_two)
    (pulled_both,) = call("pull_halo", pull_halo_kernel, cohorts, [even, age_class, speed], [fields, halo_fields, late_near, late_far, late_rims], [],
        [], [halo], [halo_fields_shape, (3, height, lon), (STEP, height, lon)], 2500, sides=(4,))

    tables = [age_class, mort_rate, crowd_coef, speed]
    partial, totals = call("backward", backward_kernel, cohorts, tables, [fields, halo_fields, crowd, crowd_two, sums, pulled, pulled_both, state, state_both],
        [density], [], [main, (9, height, lon)], [fields_shape], 5000)
    totals = total_by_halves(totals, lower)

    (shares,) = call("shares", shares_kernel, cohorts, tables, [fields, crowd, crowd_two, sums, halo_sums, pulled, pulled_both, wet_halo, state, state_both],
        [cotangent, density], [], [(6,) + tiles], [], 6000)
    shares = scatter(shares[:3] + shares[3:] * (totals[:2] * (1.0 / COH))[None], lower, first)

    (grad,) = call("last", last_kernel, cohorts, [age_class, mort_rate, crowd_coef, mass, speed],
        [totals, fields, halo_fields, crowd, partial], [], [main], [], [(3,) + tiles], 3000)

    return (grad, shares[0], shares[1], shares[2])


def solution(mesh):
    spread_spec = P("coh", None, "lat", None)
    field_spec = P(None, "lat", None)
    in_specs = (spread_spec, spread_spec) + (field_spec,) * 4 + (P("coh"),) + (P(),) * 4
    out_specs = (spread_spec,) + (P(None, "lat", "coh"),) * 3
    return jax.shard_map(local, mesh=mesh, in_specs=in_specs, out_specs=out_specs, check_vma=False)
```

```python
import functools

import jax
import jax.numpy as jnp
from jax import lax
from jax.experimental import pallas as pl
from jax.experimental.pallas import tpu as pltpu
from jax.sharding import PartitionSpec as P


COH = 128
LOG2E = 1.4426950408889634
STEP = 8
LAND = 1e7
F32 = jnp.float32


def rows_of(shape):
    return lax.broadcasted_iota(jnp.int32, shape, 0)


def turn(tile, shift):
    return pltpu.roll(tile, shift, 0)


def east(tile):
    return pltpu.roll(tile, tile.shape[1] - 1, 1)


def west(tile):
    return pltpu.roll(tile, 1, 1)


def northern(first, second, halo):
    row = rows_of(first.shape)
    return (
        jnp.where(row == 7, turn(halo, 3), turn(first, 7)),
        jnp.where(row == 7, turn(halo, 1), turn(second, 7)),
    )


def southern(first, second, halo):
    row = rows_of(first.shape)
    return (
        jnp.where(row == 0, turn(halo, 7), turn(first, 1)),
        jnp.where(row == 0, turn(halo, 5), turn(second, 1)),
    )


def within(tile, shift):
    return jnp.where(rows_of(tile.shape) == (0 if shift == 1 else 7), 0.0, turn(tile, shift))


def rim(first, second):
    row = rows_of(first.shape)
    last = jnp.where(row == 4, turn(first, 5), turn(second, 7))
    return jnp.where(row == 1, turn(first, 1), jnp.where(row == 3, turn(second, 3), last))


def halo_neighbours(own, north, south):
    row = rows_of(own.shape)
    lower, upper = (row == 1) | (row == 3), (row == 4) | (row == 6)
    return jnp.where(lower, own, turn(north, 7)), jnp.where(upper, own, turn(south, 1))


def combine(inner, added):
    row = rows_of(inner.shape)
    used = (row == 1) | (row == 3) | (row == 4) | (row == 6)
    return jnp.where(used, inner, jnp.where(row < 4, turn(added, 7), turn(added, 1)))


def addends(both):
    row = rows_of(both.shape)
    return (
        jnp.where(row == 0, both, jnp.where(row == 7, turn(both, 2), 0.0)),
        jnp.where(row == 7, both, jnp.where(row == 0, turn(both, 6), 0.0)),
    )


def stay(value):
    return pltpu.with_memory_space_constraint(value, pltpu.HBM)


def decays(mortal, crowded, crowd):
    return jnp.exp2(-LOG2E * mortal - (LOG2E / COH * crowded) * crowd)


def join(before, after, out):
    out[0:4, :] = before
    out[4:8, :] = after


def pack(source, up, down, slot):
    for out, start in ((up, 6), (down, 0)):
        out[slot, 0:2, :] = source(0, start)
        out[slot, 2:4, :] = source(1, start)


def clear(*refs):
    for ref in refs:
        ref[...] = jnp.zeros_like(ref)


def nothing():
    pass


def first_kernel(age, mass, ocean, east_vel, north_vel, kappa, state, up, down, crowd):
    cohorts = state.shape[0]

    def begin():
        clear(crowd)

    def each(group):
        for layer in range(2):
            crowd[layer] += sum(mass[age[c]] * state[c, layer] for c in group)
        for c in group:
            pack(lambda layer, start: state[c, layer, start : start + 2, :], up, down, c)

    def end():
        for slot, field in enumerate((ocean, east_vel, north_vel, kappa)):
            pack(lambda layer, start: field[layer, start : start + 2, :].astype(F32), up, down, cohorts + slot)

    return begin, each, end


def edges_kernel(state, up, down):
    def each(group):
        for c in group:
            pack(lambda layer, start: state[c, layer, start : start + 2, :], up, down, c)

    return nothing, each, nothing


def forward_kernel(age, mort, crowding, mass, speed, ocean, east_vel, north_vel, kappa, crowd, state,
                   state_out, rims, fields, crowd_out, total, sums, coef):
    def begin():
        clear(total, sums)
        for slot, (field, scale) in enumerate(((ocean, None), (east_vel, 0.5), (north_vel, 0.5), (kappa, None))):
            for layer in range(2):
                fields[slot, layer] = field[layer].astype(F32)
            if scale is not None:
                fields[slot] = scale * fields[slot]
        coef[0] = fields[0] * (1.0 - 4.0 * fields[3])
        coef[1] = fields[0] * fields[3]
        coef[2] = fields[0] * fields[1]
        coef[3] = fields[0] * fields[2]
        crowd_out[...] = jnp.where(fields[0] == 0.0, LAND, crowd[...])

    def each(group):
        for c in group:
            mortal, crowded, weight, swim = [table[age[c]] for table in (mort, crowding, mass, speed)]
            wet = [state[c, k] * decays(mortal, crowded, crowd_out[k]) for k in range(2)]
            rims[c] = rim(*wet)
            for k in range(2):
                north, south, to_east, to_west = within(wet[k], 7), within(wet[k], 1), east(wet[k]), west(wet[k])
                around = (north + south) + (to_east + to_west)
                drift = coef[2, k] * (to_east - to_west) + coef[3, k] * (north - south)
                moved = coef[0, k] * wet[k] + coef[1, k] * around - swim * drift
                state_out[c, k] = moved
                total[k] += weight * moved
                mine = weight * wet[k]
                swum = swim * mine
                sums[0, k] += mine
                sums[1, k] += swum
                sums[2, k] += crowded * mine
                sums[3, k] += crowded * swum

    return begin, each, nothing


def forward_halo_kernel(age, mort, crowding, mass, speed, fields, total, before, after, crowd_before, crowd_after, rims,
                        both_out, wet_out, halo_fields, total_out, sums, coef, own, crowd, edge, added):
    def begin():
        clear(sums, added)
        cohorts = rims.shape[0]
        for slot, scale in enumerate((None, 0.5, 0.5, None)):
            join(before[cohorts + slot], after[cohorts + slot], edge.at[0])
            halo_fields[slot] = edge[0] if scale is None else scale * edge[0]
        ocean = halo_fields[0]
        coef[0] = ocean * (1.0 - 4.0 * halo_fields[3])
        coef[1] = ocean * halo_fields[3]
        coef[2] = ocean * halo_fields[1]
        coef[3] = ocean * halo_fields[2]
        row = rows_of(ocean.shape)
        ocean = rim(fields[0, 0], fields[0, 1])
        own[0] = ocean * rim(fields[3, 0], fields[3, 1])
        own[1] = jnp.where(row < 4, ocean, -ocean) * rim(fields[2, 0], fields[2, 1])
        join(crowd_before[...], crowd_after[...], crowd)
        crowd[...] = jnp.where(halo_fields[0] == 0.0, LAND, crowd[...])

    def each(group):
        for slot, c in enumerate(group):
            join(before[c], after[c], edge.at[slot])
        for slot, c in enumerate(group):
            mortal, crowded, weight, swim = [table[age[c]] for table in (mort, crowding, mass, speed)]
            wet = edge[slot] * decays(mortal, crowded, crowd[...])
            wet_out[c] = wet
            north, south = halo_neighbours(rims[c], wet, wet)
            to_east, to_west = east(wet), west(wet)
            around = (north + south) + (to_east + to_west)
            drift = coef[2] * (to_east - to_west) + coef[3] * (north - south)
            moved = coef[0] * wet + coef[1] * around - swim * drift
            both = combine(moved, (own[0] + swim * own[1]) * wet)
            both_out[c] = both
            added[...] += weight * both
            mine = weight * wet
            sums[0] += mine
            sums[1] += swim * mine

    def end():
        total_out[2] = added[...]
        for k, more in enumerate(addends(added[...])):
            total_out[k] = total[k] + more

    return begin, each, end


def transport_coef(fields, coef):
    coef[0] = 1.0 - 4.0 * fields[3]
    coef[1] = fields[3]
    coef[2] = fields[1]
    coef[3] = fields[2]


def pull_kernel(age, speed, fields, cotangent, pulled, rims, coef):
    def begin():
        transport_coef(fields, coef)

    def each(group):
        for c in group:
            swim = speed[age[c]]
            masked = [fields[0, k] * cotangent[c, k] for k in range(2)]
            rims[c] = rim(*masked)
            for k in range(2):
                plain = coef[1, k] * masked[k]
                along = swim * (coef[3, k] * masked[k])
                across = swim * (coef[2, k] * masked[k])
                sides = east(plain + across) + west(plain - across)
                ends = within(plain + along, 7) + within(plain - along, 1)
                pulled[c, k] = fields[0, k] * (coef[0, k] * masked[k] + (ends + sides))

    return begin, each, nothing


def pull_halo_kernel(age, speed, fields, halo_fields, before, after, rims, both_out, coef, own, edge):
    def begin():
        transport_coef(halo_fields, coef)
        row = rows_of(own.shape[1:])
        side = rim(fields[2, 0], fields[2, 1])
        own[0] = rim(fields[3, 0], fields[3, 1])
        own[1] = jnp.where(row < 4, side, -side)
        own[2] = rim(fields[0, 0], fields[0, 1])

    def each(group):
        for slot, c in enumerate(group):
            join(before[c], after[c], edge.at[slot])
        for slot, c in enumerate(group):
            swim = speed[age[c]]
            masked = halo_fields[0] * edge[slot]
            plain = coef[1] * masked
            along = swim * (coef[3] * masked)
            across = swim * (coef[2] * masked)
            onward, backward = plain + along, plain - along
            sides = east(plain + across) + west(plain - across)
            north, south = halo_neighbours((own[0] + swim * own[1]) * rims[c], onward, backward)
            grad = coef[0] * masked + ((north + south) + sides)
            more = jnp.where(rows_of(grad.shape) < 4, backward, onward)
            both_out[c] = combine(halo_fields[0] * grad, own[2] * more)

    return begin, each, nothing


def whole_tiles(tiles, both, c):
    more = addends(both[c])
    return [tiles[c, 0] + more[0], tiles[c, 1] + more[1], both[c]]


def backward_kernel(age, mort, crowding, speed, fields, halo_fields, crowd, crowd_two, sums, pulled, pulled_both, state,
                    state_both, start, partial, totals, coef):
    pressure, later = totals.at[0:3], totals.at[3:5]

    def begin():
        for k in range(4):
            totals[5 + k] = sums[2 + k // 2, k % 2]
        for k in range(3):
            field = lambda n: fields[n, k] if k < 2 else halo_fields[n]
            coef[0, k] = 1.0 - 4.0 * field(3)
            coef[1, k] = field(3)
            coef[2, k] = field(1)
            coef[3, k] = field(2)
        clear(pressure, later)

    def each(group):
        for c in group:
            mortal, crowded, swim = [table[age[c]] for table in (mort, crowding, speed)]
            grad, now = whole_tiles(pulled, pulled_both, c), whole_tiles(state, state_both, c)
            value = []
            for k in range(3):
                value.append(grad[k] * decays(mortal, crowded, crowd_two[k]))
                pressure[k] -= crowded * (value[k] * now[k])
            plain = [coef[1, k] * value[k] for k in range(3)]
            along = [swim * (coef[3, k] * value[k]) for k in range(3)]
            north = northern(*[plain[k] + along[k] for k in range(3)])
            south = southern(*[plain[k] - along[k] for k in range(3)])
            for k in range(2):
                across = swim * (coef[2, k] * value[k])
                sides = east(plain[k] + across) + west(plain[k] - across)
                spread = coef[0, k] * value[k] + ((north[k] + south[k]) + sides)
                mine = decays(mortal, crowded, crowd[k]) * spread
                partial[c, k] = mine
                later[k] -= crowded * (start[c, k] * mine)

    return begin, each, nothing


def shares_kernel(age, mort, crowding, speed, fields, crowd, crowd_two, sums, halo_sums, pulled, pulled_both, wet_halo, state,
                  state_both, cotangent, start, shares):
    def begin():
        clear(shares)
        plain, swum = [[sums[n, 0], sums[n, 1], halo_sums[n]] for n in range(2)]
        plain_north, plain_south = northern(*plain), southern(*plain)
        swum_north, swum_south = northern(*swum), southern(*swum)
        for k in range(2):
            ocean = fields[0, k]
            shares[3, k] = (-0.5 * ocean) * (east(swum[k]) - west(swum[k]))
            shares[4, k] = (-0.5 * ocean) * (swum_north[k] - swum_south[k])
            around = plain_north[k] + plain_south[k] + east(plain[k]) + west(plain[k])
            shares[5, k] = ocean * (around - 4.0 * plain[k])

    def each(group):
        for c in group:
            mortal, crowded, swim = [table[age[c]] for table in (mort, crowding, speed)]
            old = [start[c, k] * decays(mortal, crowded, crowd[k]) for k in range(2)] + [wet_halo[c]]
            fade = [decays(mortal, crowded, crowd_two[k]) for k in range(3)]
            new = [tile * fade[k] for k, tile in enumerate(whole_tiles(state, state_both, c))]
            grad = whole_tiles(pulled, pulled_both, c)
            for wet, weigh in ((old, lambda k: grad[k] * fade[k]), (new, lambda k: fields[0, k] * cotangent[c, k])):
                north, south = northern(*wet), southern(*wet)
                for k in range(2):
                    by = weigh(k)
                    to_east, to_west = east(wet[k]), west(wet[k])
                    pace = (-0.5 * swim) * by
                    shares[0, k] += pace * (to_east - to_west)
                    shares[1, k] += pace * (north[k] - south[k])
                    shares[2, k] += by * ((north[k] + south[k]) + (to_east + to_west) - 4.0 * wet[k])

    return begin, each, nothing


def last_kernel(age, mort, crowding, mass, speed, totals, fields, halo_fields, crowd, partial, out, terms):
    pressure = totals.at[0:3]

    def begin():
        field = lambda n, k: fields[n, k] if k < 2 else halo_fields[n]
        value = [field(0, k) * (pressure[k] * (1.0 / COH)) for k in range(3)]
        plain = [field(3, k) * value[k] for k in range(3)]
        along = [field(2, k) * value[k] for k in range(3)]
        north, south = northern(*plain), southern(*plain)
        drift_north, drift_south = northern(*along), southern(*along)
        for k in range(2):
            across = fields[1, k] * value[k]
            still = (1.0 - 4.0 * fields[3, k]) * value[k]
            still += (north[k] + south[k]) + (east(plain[k]) + west(plain[k]))
            moving = (drift_north[k] - drift_south[k]) + (east(across) - west(across))
            terms[0, k] = still
            terms[1, k] = moving
            terms[2, k] = (totals[3 + k] - totals[5 + k] * still - totals[7 + k] * moving) * (1.0 / COH)

    def each(group):
        for c in group:
            mortal, crowded, weight, swim = [table[age[c]] for table in (mort, crowding, mass, speed)]
            for k in range(2):
                term = decays(mortal, crowded, crowd[k]) * (terms[0, k] + swim * terms[1, k]) + terms[2, k]
                out[c, k] = partial[c, k] + weight * term

    return begin, each, nothing


def driver(kernel, cohorts, sides, n_tables, n_small, n_in, n_out, n_whole, n_scratch, *refs):
    refs = list(refs)

    def take(count):
        taken, refs[:] = refs[:count], refs[count:]
        return taken

    tables = take(n_tables)
    small, sources, sinks, wholes, scratch = take(n_small), take(n_in), take(n_out), take(n_whole), take(n_scratch)
    inside, outside, held = take(n_in), take(n_out), take(n_tables)
    table_sem = refs.pop()
    lookups = [pltpu.make_async_copy(a, b, table_sem.at[n]) for n, (a, b) in enumerate(zip(tables, held))]
    for copy in lookups:
        copy.start()
    groups = cohorts // STEP

    def span(group):
        return pl.ds(pl.multiple_of(group * STEP, STEP) if not isinstance(group, int) else group * STEP, STEP)

    def loads(group):
        return [pltpu.make_async_copy(a.at[span(group)], b.at[span(group)], refs[0].at[n, group])
                for n, (a, b) in enumerate(zip(sources, inside))]

    def stores(group):
        return [pltpu.make_async_copy(b.at[span(group)], a.at[span(group)], refs[-1].at[n, group])
                for n, (a, b) in enumerate(zip(sinks, outside))]

    for group in range(groups):
        for copy in loads(group):
            copy.start()

    for copy in lookups:
        copy.wait()

    def run(arrays):
        begin, each, end = kernel(*arrays)
        begin()

        def step(group, _):
            for copy in loads(group):
                copy.wait()
            each([group * STEP + slot for slot in range(STEP)])
            for copy in stores(group):
                copy.start()
            return 0

        lax.fori_loop(0, groups, step, 0)
        end()

    arrays = held + small + inside + outside + wholes + scratch
    n_small += n_tables
    if sides is None:
        run(arrays)
    else:
        even, arrays = arrays[0], arrays[1:]
        turned = list(arrays)
        for side in sides:
            turned[side], turned[side + 1] = arrays[side + 1], arrays[side]

        @pl.when(even[0] == 1)
        def _():
            run(turned if sides[0] < n_small else arrays)

        @pl.when(even[0] == 0)
        def _():
            run(arrays if sides[0] < n_small else turned)

    for group in range(groups):
        for copy in stores(group):
            copy.wait()


VMEM_BYTES = {"first": 8, "late_edges": 6, "forward": 8, "pull": 8, "forward_halo": 8, "pull_halo": 8, "backward": 8,
              "shares": 10, "last": 8}
VMEM = pl.BlockSpec(memory_space=pltpu.VMEM)
LARGE = pl.BlockSpec(memory_space=pl.ANY)


def call(name, kernel, cohorts, tables, small, large, large_outs, outs, scratch, cycles, sides=None):
    groups = cohorts // STEP
    vmem = lambda shape: pltpu.VMEM(shape, F32)
    sems = [pltpu.SemaphoreType.DMA((len(arrays), groups)) for arrays in (large, large_outs) if arrays]
    outputs = pl.pallas_call(
        functools.partial(driver, kernel, cohorts, sides, len(tables), len(small), len(large), len(large_outs), len(outs), len(scratch)),
        in_specs=[LARGE] * len(tables) + [VMEM] * len(small) + [LARGE] * len(large),
        out_specs=[LARGE] * len(large_outs) + [VMEM] * len(outs),
        out_shape=[pltpu.HBM(shape, F32) for shape in large_outs] + [jax.ShapeDtypeStruct(shape, F32) for shape in outs],
        scratch_shapes=[vmem(shape) for shape in scratch] + [vmem(x.shape) for x in large]
        + [vmem(shape) for shape in large_outs] + [(pltpu.SMEM if x.ndim == 1 else pltpu.VMEM)(x.shape, x.dtype) for x in tables]
        + sems + [pltpu.SemaphoreType.DMA((len(tables),))],
        compiler_params=pltpu.CompilerParams(vmem_limit_bytes=VMEM_BYTES[name] << 20),
        cost_estimate=pl.CostEstimate(flops=cycles, transcendentals=0, bytes_accessed=cycles),
    )(*[stay(x) for x in tables], *small, *[stay(x) for x in large])
    count = len(large_outs)
    return [stay(x) for x in outputs[:count]] + list(outputs[count:])


def swap(value, flip):
    return lax.ppermute(value, "coh", [(i, i ^ flip) for i in range(4)])


def total_of(value):
    value = value + swap(value, 1)
    return value + swap(value, 2)


def total_by_halves(value, lower):
    middle = value.shape[-1] // 2
    low, high = value[..., :middle], value[..., middle:]
    keep, send = jnp.where(lower, low, high), jnp.where(lower, high, low)
    keep = keep + swap(send, 1)
    keep = keep + swap(keep, 2)
    other = swap(keep, 1)
    return jnp.where(lower, jnp.concatenate([keep, other], -1), jnp.concatenate([other, keep], -1))


def own_quarters(value, lower):
    fourth = value.shape[-1] // 4
    parts = [value[..., k * fourth : (k + 1) * fourth] for k in range(4)]
    keep = jnp.stack([jnp.where(lower, parts[2 * k], parts[2 * k + 1]) for k in range(2)])
    send = jnp.stack([jnp.where(lower, parts[2 * k + 1], parts[2 * k]) for k in range(2)])
    return keep, send


def near_swap(value, count):
    return lax.ppermute(value, "lat", [(i, i ^ 1) for i in range(count)])


def far_swap(value, count):
    return lax.ppermute(value, "lat", [(i, ((i + 1) ^ 1) - 1) for i in range(1, count - 1)])


def local(density, cotangent, land_mask, east_vel, north_vel, diffusion, age_class, mort_rate, crowd_coef, mass, speed):
    age_class, mort_rate, crowd_coef, mass, speed = [stay(x) for x in (age_class, mort_rate, crowd_coef, mass, speed)]
    raw_fields = [stay(x) for x in (land_mask, east_vel, north_vel, diffusion)]
    count = lax.axis_size("lat")
    strip, group = lax.axis_index("lat") & 1, lax.axis_index("coh")
    choices = (1 - strip).astype(jnp.int32)[None], strip == 1, (group & 1) == 0, (group & 2) == 0
    density, (even, odd, lower, first) = lax.optimization_barrier((density, choices))
    cohorts, _, height, lon = density.shape
    main, halo, edge = (cohorts, 2, height, lon), (cohorts, height, lon), (cohorts, 4, lon)
    tiles, three, fields_shape = (2, height, lon), (3, height, lon), (4, 3, height, lon)

    wide = (cohorts + 4, 4, lon)
    near, far, crowd = call("first", first_kernel, cohorts, [even, age_class, mass] + raw_fields, [], [density], [], [wide, wide, tiles], [],
                            2000, sides=(len(raw_fields) + 3,))
    crowd = total_of(crowd)
    late_near, late_far = call("late_edges", edges_kernel, cohorts, [even], [], [cotangent], [], [edge, edge], [], 2000, sides=(1,))

    def edge_rows(value, start):
        return value[:, start : start + 2].reshape(4, lon)

    up, down = edge_rows(crowd, height - 2), edge_rows(crowd, 0)
    crowd_far = far_swap(jnp.where(odd, up, down), count)
    crowd_near = near_swap(jnp.where(odd, down, up), count)
    far = far_swap(far, count)
    near = near_swap(near, count)
    late_far = far_swap(late_far, count)
    late_near = near_swap(late_near, count)

    tables = [age_class, mort_rate, crowd_coef, mass, speed]
    own_fields, halo_fields_shape = (4,) + tiles, (4, height, lon)
    state, rims, fields, crowd, crowd_two, sums = call("forward", forward_kernel, cohorts, tables + raw_fields, [crowd], [density],
        [], [main, halo, own_fields, tiles, tiles, (4,) + tiles], [own_fields], 4000)
    pulled, late_rims = call("pull", pull_kernel, cohorts, [age_class, speed], [fields], [cotangent], [], [main, halo], [own_fields], 4000)
    state_both, wet_halo, halo_fields, crowd_two, halo_sums = call("forward_halo", forward_halo_kernel, cohorts, [even] + tables, [fields, crowd_two, near, far, crowd_near, crowd_far, rims], [],
        [], [halo, halo, halo_fields_shape, three, (2, height, lon)],
        [halo_fields_shape, (2, height, lon), (height, lon), (STEP, height, lon), (height, lon)], 2500, sides=(7, 9))
    crowd_two = total_of(crowd_two)
    (pulled_both,) = call("pull_halo", pull_halo_kernel, cohorts, [even, age_class, speed], [fields, halo_fields, late_near, late_far, late_rims], [],
        [], [halo], [halo_fields_shape, (3, height, lon), (STEP, height, lon)], 2500, sides=(4,))

    tables = [age_class, mort_rate, crowd_coef, speed]
    partial, totals = call("backward", backward_kernel, cohorts, tables, [fields, halo_fields, crowd, crowd_two, sums, pulled, pulled_both, state, state_both],
        [density], [], [main, (9, height, lon)], [fields_shape], 5000)
    totals = total_by_halves(totals, lower)

    (shares,) = call("shares", shares_kernel, cohorts, tables, [fields, crowd, crowd_two, sums, halo_sums, pulled, pulled_both, wet_halo, state, state_both],
        [cotangent, density], [], [(6,) + tiles], [], 6000)
    keep, send = own_quarters(shares, lower)
    keep = keep + swap(send, 1)
    scale, _ = own_quarters(totals[:2] * (1.0 / COH), lower)
    keep = keep[:, :3] + keep[:, 3:] * scale[:, None]
    mine, rest = jnp.where(first, keep[0], keep[1]), jnp.where(first, keep[1], keep[0])
    shares = mine + swap(rest, 2)

    (grad,) = call("last", last_kernel, cohorts, [age_class, mort_rate, crowd_coef, mass, speed],
        [totals, fields, halo_fields, crowd, partial], [], [main], [], [(3,) + tiles], 3000)

    return (grad, shares[0], shares[1], shares[2])


def solution(mesh):
    spread_spec = P("coh", None, "lat", None)
    field_spec = P(None, "lat", None)
    in_specs = (spread_spec, spread_spec) + (field_spec,) * 4 + (P("coh"),) + (P(),) * 4
    out_specs = (spread_spec,) + (P(None, "lat", "coh"),) * 3
    return jax.shard_map(local, mesh=mesh, in_specs=in_specs, out_specs=out_specs, check_vma=False)
```

```python
import functools

import jax
import jax.numpy as jnp
from jax import lax
from jax.experimental import pallas as pl
from jax.experimental.pallas import tpu as pltpu
from jax.sharding import PartitionSpec as P


COH = 128
LOG2E = 1.4426950408889634
STEP = 8
LAND = 1e7
F32 = jnp.float32


def rows_of(shape):
    return lax.broadcasted_iota(jnp.int32, shape, 0)


def turn(tile, shift):
    return pltpu.roll(tile, shift, 0)


def east(tile):
    return pltpu.roll(tile, tile.shape[1] - 1, 1)


def west(tile):
    return pltpu.roll(tile, 1, 1)


def northern(first, second, halo):
    row = rows_of(first.shape)
    return (
        jnp.where(row == 7, turn(halo, 3), turn(first, 7)),
        jnp.where(row == 7, turn(halo, 1), turn(second, 7)),
    )


def southern(first, second, halo):
    row = rows_of(first.shape)
    return (
        jnp.where(row == 0, turn(halo, 7), turn(first, 1)),
        jnp.where(row == 0, turn(halo, 5), turn(second, 1)),
    )


def within(tile, shift):
    return jnp.where(rows_of(tile.shape) == (0 if shift == 1 else 7), 0.0, turn(tile, shift))


def rim(first, second):
    row = rows_of(first.shape)
    last = jnp.where(row == 4, turn(first, 5), turn(second, 7))
    return jnp.where(row == 1, turn(first, 1), jnp.where(row == 3, turn(second, 3), last))


def halo_neighbours(own, north, south):
    row = rows_of(own.shape)
    lower, upper = (row == 1) | (row == 3), (row == 4) | (row == 6)
    return jnp.where(lower, own, turn(north, 7)), jnp.where(upper, own, turn(south, 1))


def combine(inner, added):
    row = rows_of(inner.shape)
    used = (row == 1) | (row == 3) | (row == 4) | (row == 6)
    return jnp.where(used, inner, jnp.where(row < 4, turn(added, 7), turn(added, 1)))


def addends(both):
    row = rows_of(both.shape)
    return (
        jnp.where(row == 0, both, jnp.where(row == 7, turn(both, 2), 0.0)),
        jnp.where(row == 7, both, jnp.where(row == 0, turn(both, 6), 0.0)),
    )


def stay(value):
    return pltpu.with_memory_space_constraint(value, pltpu.HBM)


def decays(mortal, crowded, crowd):
    return jnp.exp2(-LOG2E * mortal - (LOG2E / COH * crowded) * crowd)


def join(before, after, out):
    out[0:4, :] = before
    out[4:8, :] = after


def pack(source, up, down, slot):
    for out, start in ((up, 6), (down, 0)):
        out[slot, 0:2, :] = source(0, start)
        out[slot, 2:4, :] = source(1, start)


def clear(*refs):
    for ref in refs:
        ref[...] = jnp.zeros_like(ref)


def nothing():
    pass


def first_kernel(age, mass, ocean, east_vel, north_vel, kappa, state, up, down, crowd):
    cohorts = state.shape[0]

    def begin():
        clear(crowd)

    def each(group):
        for layer in range(2):
            crowd[layer] += sum(mass[age[c]] * state[c, layer] for c in group)
        for c in group:
            pack(lambda layer, start: state[c, layer, start : start + 2, :], up, down, c)

    def end():
        for slot, field in enumerate((ocean, east_vel, north_vel, kappa)):
            pack(lambda layer, start: field[layer, start : start + 2, :].astype(F32), up, down, cohorts + slot)

    return begin, each, end


def edges_kernel(state, up, down):
    def each(group):
        for c in group:
            pack(lambda layer, start: state[c, layer, start : start + 2, :], up, down, c)

    return nothing, each, nothing


def forward_kernel(age, mort, crowding, mass, speed, ocean, east_vel, north_vel, kappa, crowd, state,
                   state_out, rims, fields, crowd_out, total, sums, coef):
    def begin():
        clear(total, sums)
        for slot, (field, scale) in enumerate(((ocean, None), (east_vel, 0.5), (north_vel, 0.5), (kappa, None))):
            for layer in range(2):
                fields[slot, layer] = field[layer].astype(F32)
            if scale is not None:
                fields[slot] = scale * fields[slot]
        coef[0] = fields[0] * (1.0 - 4.0 * fields[3])
        coef[1] = fields[0] * fields[3]
        coef[2] = fields[0] * fields[1]
        coef[3] = fields[0] * fields[2]
        crowd_out[...] = jnp.where(fields[0] == 0.0, LAND, crowd[...])

    def each(group):
        for c in group:
            mortal, crowded, weight, swim = [table[age[c]] for table in (mort, crowding, mass, speed)]
            wet = [state[c, k] * decays(mortal, crowded, crowd_out[k]) for k in range(2)]
            rims[c] = rim(*wet)
            for k in range(2):
                north, south, to_east, to_west = within(wet[k], 7), within(wet[k], 1), east(wet[k]), west(wet[k])
                around = (north + south) + (to_east + to_west)
                drift = coef[2, k] * (to_east - to_west) + coef[3, k] * (north - south)
                moved = coef[0, k] * wet[k] + coef[1, k] * around - swim * drift
                state_out[c, k] = moved
                total[k] += weight * moved
                mine = weight * wet[k]
                swum = swim * mine
                sums[0, k] += mine
                sums[1, k] += swum
                sums[2, k] += crowded * mine
                sums[3, k] += crowded * swum

    return begin, each, nothing


def forward_halo_kernel(age, mort, crowding, mass, speed, fields, total, before, after, crowd_before, crowd_after, rims,
                        both_out, wet_out, halo_fields, total_out, sums, coef, own, crowd, edge, added):
    def begin():
        clear(sums, added)
        cohorts = rims.shape[0]
        for slot, scale in enumerate((None, 0.5, 0.5, None)):
            join(before[cohorts + slot], after[cohorts + slot], edge.at[0])
            halo_fields[slot] = edge[0] if scale is None else scale * edge[0]
        ocean = halo_fields[0]
        coef[0] = ocean * (1.0 - 4.0 * halo_fields[3])
        coef[1] = ocean * halo_fields[3]
        coef[2] = ocean * halo_fields[1]
        coef[3] = ocean * halo_fields[2]
        row = rows_of(ocean.shape)
        ocean = rim(fields[0, 0], fields[0, 1])
        own[0] = ocean * rim(fields[3, 0], fields[3, 1])
        own[1] = jnp.where(row < 4, ocean, -ocean) * rim(fields[2, 0], fields[2, 1])
        join(crowd_before[...], crowd_after[...], crowd)
        crowd[...] = jnp.where(halo_fields[0] == 0.0, LAND, crowd[...])

    def each(group):
        for slot, c in enumerate(group):
            join(before[c], after[c], edge.at[slot])
        for slot, c in enumerate(group):
            mortal, crowded, weight, swim = [table[age[c]] for table in (mort, crowding, mass, speed)]
            wet = edge[slot] * decays(mortal, crowded, crowd[...])
            wet_out[c] = wet
            north, south = halo_neighbours(rims[c], wet, wet)
            to_east, to_west = east(wet), west(wet)
            around = (north + south) + (to_east + to_west)
            drift = coef[2] * (to_east - to_west) + coef[3] * (north - south)
            moved = coef[0] * wet + coef[1] * around - swim * drift
            both = combine(moved, (own[0] + swim * own[1]) * wet)
            both_out[c] = both
            added[...] += weight * both
            mine = weight * wet
            sums[0] += mine
            sums[1] += swim * mine

    def end():
        total_out[2] = added[...]
        for k, more in enumerate(addends(added[...])):
            total_out[k] = total[k] + more

    return begin, each, end


def transport_coef(fields, coef):
    coef[0] = 1.0 - 4.0 * fields[3]
    coef[1] = fields[3]
    coef[2] = fields[1]
    coef[3] = fields[2]


def pull_kernel(age, speed, fields, cotangent, pulled, rims, coef):
    def begin():
        transport_coef(fields, coef)

    def each(group):
        for c in group:
            swim = speed[age[c]]
            masked = [fields[0, k] * cotangent[c, k] for k in range(2)]
            rims[c] = rim(*masked)
            for k in range(2):
                plain = coef[1, k] * masked[k]
                along = swim * (coef[3, k] * masked[k])
                across = swim * (coef[2, k] * masked[k])
                sides = east(plain + across) + west(plain - across)
                ends = within(plain + along, 7) + within(plain - along, 1)
                pulled[c, k] = fields[0, k] * (coef[0, k] * masked[k] + (ends + sides))

    return begin, each, nothing


def pull_halo_kernel(age, speed, fields, halo_fields, before, after, rims, both_out, coef, own, edge):
    def begin():
        transport_coef(halo_fields, coef)
        row = rows_of(own.shape[1:])
        side = rim(fields[2, 0], fields[2, 1])
        own[0] = rim(fields[3, 0], fields[3, 1])
        own[1] = jnp.where(row < 4, side, -side)
        own[2] = rim(fields[0, 0], fields[0, 1])

    def each(group):
        for slot, c in enumerate(group):
            join(before[c], after[c], edge.at[slot])
        for slot, c in enumerate(group):
            swim = speed[age[c]]
            masked = halo_fields[0] * edge[slot]
            plain = coef[1] * masked
            along = swim * (coef[3] * masked)
            across = swim * (coef[2] * masked)
            onward, backward = plain + along, plain - along
            sides = east(plain + across) + west(plain - across)
            north, south = halo_neighbours((own[0] + swim * own[1]) * rims[c], onward, backward)
            grad = coef[0] * masked + ((north + south) + sides)
            more = jnp.where(rows_of(grad.shape) < 4, backward, onward)
            both_out[c] = combine(halo_fields[0] * grad, own[2] * more)

    return begin, each, nothing


def whole_tiles(tiles, both, c):
    more = addends(both[c])
    return [tiles[c, 0] + more[0], tiles[c, 1] + more[1], both[c]]


def backward_kernel(age, mort, crowding, speed, fields, halo_fields, crowd, crowd_two, sums, pulled, pulled_both, state,
                    state_both, start, partial, totals, value_out, faded_out, faded_halo, coef):
    pressure, later = totals.at[0:3], totals.at[3:5]

    def begin():
        for k in range(4):
            totals[5 + k] = sums[2 + k // 2, k % 2]
        for k in range(3):
            field = lambda n: fields[n, k] if k < 2 else halo_fields[n]
            coef[0, k] = 1.0 - 4.0 * field(3)
            coef[1, k] = field(3)
            coef[2, k] = field(1)
            coef[3, k] = field(2)
        clear(pressure, later)

    def each(group):
        for c in group:
            mortal, crowded, swim = [table[age[c]] for table in (mort, crowding, speed)]
            grad, now = whole_tiles(pulled, pulled_both, c), whole_tiles(state, state_both, c)
            value = []
            for k in range(3):
                fade = decays(mortal, crowded, crowd_two[k])
                value.append(grad[k] * fade)
                if k < 2:
                    value_out[c, k] = value[k]
                    faded_out[c, k] = now[k] * fade
                else:
                    faded_halo[c] = now[k] * fade
                pressure[k] -= crowded * (value[k] * now[k])
            plain = [coef[1, k] * value[k] for k in range(3)]
            along = [swim * (coef[3, k] * value[k]) for k in range(3)]
            north = northern(*[plain[k] + along[k] for k in range(3)])
            south = southern(*[plain[k] - along[k] for k in range(3)])
            for k in range(2):
                across = swim * (coef[2, k] * value[k])
                sides = east(plain[k] + across) + west(plain[k] - across)
                spread = coef[0, k] * value[k] + ((north[k] + south[k]) + sides)
                mine = decays(mortal, crowded, crowd[k]) * spread
                partial[c, k] = mine
                later[k] -= crowded * (start[c, k] * mine)

    return begin, each, nothing


def shares_kernel(age, mort, crowding, speed, fields, crowd, sums, halo_sums, value, faded, faded_halo, wet_halo,
                  cotangent, start, shares):
    def begin():
        clear(shares)
        plain, swum = [[sums[n, 0], sums[n, 1], halo_sums[n]] for n in range(2)]
        plain_north, plain_south = northern(*plain), southern(*plain)
        swum_north, swum_south = northern(*swum), southern(*swum)
        for k in range(2):
            ocean = fields[0, k]
            shares[3, k] = (-0.5 * ocean) * (east(swum[k]) - west(swum[k]))
            shares[4, k] = (-0.5 * ocean) * (swum_north[k] - swum_south[k])
            around = plain_north[k] + plain_south[k] + east(plain[k]) + west(plain[k])
            shares[5, k] = ocean * (around - 4.0 * plain[k])

    def each(group):
        for c in group:
            mortal, crowded, swim = [table[age[c]] for table in (mort, crowding, speed)]
            old = [start[c, k] * decays(mortal, crowded, crowd[k]) for k in range(2)] + [wet_halo[c]]
            new = [faded[c, 0], faded[c, 1], faded_halo[c]]
            for wet, weigh in ((old, lambda k: value[c, k]), (new, lambda k: fields[0, k] * cotangent[c, k])):
                north, south = northern(*wet), southern(*wet)
                for k in range(2):
                    by = weigh(k)
                    to_east, to_west = east(wet[k]), west(wet[k])
                    pace = (-0.5 * swim) * by
                    shares[0, k] += pace * (to_east - to_west)
                    shares[1, k] += pace * (north[k] - south[k])
                    shares[2, k] += by * ((north[k] + south[k]) + (to_east + to_west) - 4.0 * wet[k])

    return begin, each, nothing


def last_kernel(age, mort, crowding, mass, speed, totals, fields, halo_fields, crowd, partial, out, terms):
    pressure = totals.at[0:3]

    def begin():
        field = lambda n, k: fields[n, k] if k < 2 else halo_fields[n]
        value = [field(0, k) * (pressure[k] * (1.0 / COH)) for k in range(3)]
        plain = [field(3, k) * value[k] for k in range(3)]
        along = [field(2, k) * value[k] for k in range(3)]
        north, south = northern(*plain), southern(*plain)
        drift_north, drift_south = northern(*along), southern(*along)
        for k in range(2):
            across = fields[1, k] * value[k]
            still = (1.0 - 4.0 * fields[3, k]) * value[k]
            still += (north[k] + south[k]) + (east(plain[k]) + west(plain[k]))
            moving = (drift_north[k] - drift_south[k]) + (east(across) - west(across))
            terms[0, k] = still
            terms[1, k] = moving
            terms[2, k] = (totals[3 + k] - totals[5 + k] * still - totals[7 + k] * moving) * (1.0 / COH)

    def each(group):
        for c in group:
            mortal, crowded, weight, swim = [table[age[c]] for table in (mort, crowding, mass, speed)]
            for k in range(2):
                term = decays(mortal, crowded, crowd[k]) * (terms[0, k] + swim * terms[1, k]) + terms[2, k]
                out[c, k] = partial[c, k] + weight * term

    return begin, each, nothing


def driver(kernel, cohorts, sides, n_tables, n_small, n_in, n_out, n_whole, n_scratch, *refs):
    refs = list(refs)

    def take(count):
        taken, refs[:] = refs[:count], refs[count:]
        return taken

    tables = take(n_tables)
    small, sources, sinks, wholes, scratch = take(n_small), take(n_in), take(n_out), take(n_whole), take(n_scratch)
    inside, outside, held = take(n_in), take(n_out), take(n_tables)
    table_sem = refs.pop()
    lookups = [pltpu.make_async_copy(a, b, table_sem.at[n]) for n, (a, b) in enumerate(zip(tables, held))]
    for copy in lookups:
        copy.start()
    groups = cohorts // STEP

    def span(group):
        return pl.ds(pl.multiple_of(group * STEP, STEP) if not isinstance(group, int) else group * STEP, STEP)

    def loads(group):
        return [pltpu.make_async_copy(a.at[span(group)], b.at[span(group)], refs[0].at[n, group])
                for n, (a, b) in enumerate(zip(sources, inside))]

    def stores(group):
        return [pltpu.make_async_copy(b.at[span(group)], a.at[span(group)], refs[-1].at[n, group])
                for n, (a, b) in enumerate(zip(sinks, outside))]

    for group in range(groups):
        for copy in loads(group):
            copy.start()

    for copy in lookups:
        copy.wait()

    def run(arrays):
        begin, each, end = kernel(*arrays)
        begin()

        def step(group, _):
            for copy in loads(group):
                copy.wait()
            each([group * STEP + slot for slot in range(STEP)])
            for copy in stores(group):
                copy.start()
            return 0

        lax.fori_loop(0, groups, step, 0)
        end()

    arrays = held + small + inside + outside + wholes + scratch
    n_small += n_tables
    if sides is None:
        run(arrays)
    else:
        even, arrays = arrays[0], arrays[1:]
        turned = list(arrays)
        for side in sides:
            turned[side], turned[side + 1] = arrays[side + 1], arrays[side]

        @pl.when(even[0] == 1)
        def _():
            run(turned if sides[0] < n_small else arrays)

        @pl.when(even[0] == 0)
        def _():
            run(arrays if sides[0] < n_small else turned)

    for group in range(groups):
        for copy in stores(group):
            copy.wait()


VMEM_BYTES = {"first": 8, "late_edges": 6, "forward": 8, "pull": 8, "forward_halo": 8, "pull_halo": 8, "backward": 8,
              "shares": 10, "last": 8}
VMEM = pl.BlockSpec(memory_space=pltpu.VMEM)
LARGE = pl.BlockSpec(memory_space=pl.ANY)


def call(name, kernel, cohorts, tables, small, large, large_outs, outs, scratch, cycles, sides=None):
    groups = cohorts // STEP
    vmem = lambda shape: pltpu.VMEM(shape, F32)
    sems = [pltpu.SemaphoreType.DMA((len(arrays), groups)) for arrays in (large, large_outs) if arrays]
    outputs = pl.pallas_call(
        functools.partial(driver, kernel, cohorts, sides, len(tables), len(small), len(large), len(large_outs), len(outs), len(scratch)),
        in_specs=[LARGE] * len(tables) + [VMEM] * len(small) + [LARGE] * len(large),
        out_specs=[LARGE] * len(large_outs) + [VMEM] * len(outs),
        out_shape=[pltpu.HBM(shape, F32) for shape in large_outs] + [jax.ShapeDtypeStruct(shape, F32) for shape in outs],
        scratch_shapes=[vmem(shape) for shape in scratch] + [vmem(x.shape) for x in large]
        + [vmem(shape) for shape in large_outs] + [(pltpu.SMEM if x.ndim == 1 else pltpu.VMEM)(x.shape, x.dtype) for x in tables]
        + sems + [pltpu.SemaphoreType.DMA((len(tables),))],
        compiler_params=pltpu.CompilerParams(vmem_limit_bytes=VMEM_BYTES[name] << 20),
        cost_estimate=pl.CostEstimate(flops=cycles, transcendentals=0, bytes_accessed=cycles),
    )(*[stay(x) for x in tables], *small, *[stay(x) for x in large])
    count = len(large_outs)
    return [stay(x) for x in outputs[:count]] + list(outputs[count:])


def swap(value, flip):
    return lax.ppermute(value, "coh", [(i, i ^ flip) for i in range(4)])


def total_of(value):
    value = value + swap(value, 1)
    return value + swap(value, 2)


def total_by_halves(value, lower):
    middle = value.shape[-1] // 2
    low, high = value[..., :middle], value[..., middle:]
    keep, send = jnp.where(lower, low, high), jnp.where(lower, high, low)
    keep = keep + swap(send, 1)
    keep = keep + swap(keep, 2)
    other = swap(keep, 1)
    return jnp.where(lower, jnp.concatenate([keep, other], -1), jnp.concatenate([other, keep], -1))


def own_quarters(value, lower):
    fourth = value.shape[-1] // 4
    parts = [value[..., k * fourth : (k + 1) * fourth] for k in range(4)]
    keep = jnp.stack([jnp.where(lower, parts[2 * k], parts[2 * k + 1]) for k in range(2)])
    send = jnp.stack([jnp.where(lower, parts[2 * k + 1], parts[2 * k]) for k in range(2)])
    return keep, send


def near_swap(value, count):
    return lax.ppermute(value, "lat", [(i, i ^ 1) for i in range(count)])


def far_swap(value, count):
    return lax.ppermute(value, "lat", [(i, ((i + 1) ^ 1) - 1) for i in range(1, count - 1)])


def local(density, cotangent, land_mask, east_vel, north_vel, diffusion, age_class, mort_rate, crowd_coef, mass, speed):
    age_class, mort_rate, crowd_coef, mass, speed = [stay(x) for x in (age_class, mort_rate, crowd_coef, mass, speed)]
    raw_fields = [stay(x) for x in (land_mask, east_vel, north_vel, diffusion)]
    count = lax.axis_size("lat")
    strip, group = lax.axis_index("lat") & 1, lax.axis_index("coh")
    choices = (1 - strip).astype(jnp.int32)[None], strip == 1, (group & 1) == 0, (group & 2) == 0
    density, (even, odd, lower, first) = lax.optimization_barrier((density, choices))
    cohorts, _, height, lon = density.shape
    main, halo, edge = (cohorts, 2, height, lon), (cohorts, height, lon), (cohorts, 4, lon)
    tiles, three, fields_shape = (2, height, lon), (3, height, lon), (4, 3, height, lon)

    wide = (cohorts + 4, 4, lon)
    near, far, crowd = call("first", first_kernel, cohorts, [even, age_class, mass] + raw_fields, [], [density], [], [wide, wide, tiles], [],
                            2000, sides=(len(raw_fields) + 3,))
    crowd = total_of(crowd)
    late_near, late_far = call("late_edges", edges_kernel, cohorts, [even], [], [cotangent], [], [edge, edge], [], 2000, sides=(1,))

    def edge_rows(value, start):
        return value[:, start : start + 2].reshape(4, lon)

    up, down = edge_rows(crowd, height - 2), edge_rows(crowd, 0)
    crowd_far = far_swap(jnp.where(odd, up, down), count)
    crowd_near = near_swap(jnp.where(odd, down, up), count)
    far = far_swap(far, count)
    near = near_swap(near, count)
    late_far = far_swap(late_far, count)
    late_near = near_swap(late_near, count)

    tables = [age_class, mort_rate, crowd_coef, mass, speed]
    own_fields, halo_fields_shape = (4,) + tiles, (4, height, lon)
    state, rims, fields, crowd, crowd_two, sums = call("forward", forward_kernel, cohorts, tables + raw_fields, [crowd], [density],
        [], [main, halo, own_fields, tiles, tiles, (4,) + tiles], [own_fields], 4000)
    pulled, late_rims = call("pull", pull_kernel, cohorts, [age_class, speed], [fields], [cotangent], [], [main, halo], [own_fields], 4000)
    state_both, wet_halo, halo_fields, crowd_two, halo_sums = call("forward_halo", forward_halo_kernel, cohorts, [even] + tables, [fields, crowd_two, near, far, crowd_near, crowd_far, rims], [],
        [], [halo, halo, halo_fields_shape, three, (2, height, lon)],
        [halo_fields_shape, (2, height, lon), (height, lon), (STEP, height, lon), (height, lon)], 2500, sides=(7, 9))
    crowd_two = total_of(crowd_two)
    (pulled_both,) = call("pull_halo", pull_halo_kernel, cohorts, [even, age_class, speed], [fields, halo_fields, late_near, late_far, late_rims], [],
        [], [halo], [halo_fields_shape, (3, height, lon), (STEP, height, lon)], 2500, sides=(4,))

    tables = [age_class, mort_rate, crowd_coef, speed]
    partial, totals, value, faded, faded_halo = call("backward", backward_kernel, cohorts, tables, [fields, halo_fields, crowd, crowd_two, sums, pulled, pulled_both, state, state_both],
        [density], [], [main, (9, height, lon), main, main, halo], [fields_shape], 5000)
    totals = total_by_halves(totals, lower)

    (shares,) = call("shares", shares_kernel, cohorts, tables, [fields, crowd, sums, halo_sums, value, faded, faded_halo, wet_halo],
        [cotangent, density], [], [(6,) + tiles], [], 6000)
    keep, send = own_quarters(shares, lower)
    keep = keep + swap(send, 1)
    scale, _ = own_quarters(totals[:2] * (1.0 / COH), lower)
    keep = keep[:, :3] + keep[:, 3:] * scale[:, None]
    mine, rest = jnp.where(first, keep[0], keep[1]), jnp.where(first, keep[1], keep[0])
    shares = mine + swap(rest, 2)

    (grad,) = call("last", last_kernel, cohorts, [age_class, mort_rate, crowd_coef, mass, speed],
        [totals, fields, halo_fields, crowd, partial], [], [main], [], [(3,) + tiles], 3000)

    return (grad, shares[0], shares[1], shares[2])


def solution(mesh):
    spread_spec = P("coh", None, "lat", None)
    field_spec = P(None, "lat", None)
    in_specs = (spread_spec, spread_spec) + (field_spec,) * 4 + (P("coh"),) + (P(),) * 4
    out_specs = (spread_spec,) + (P(None, "lat", "coh"),) * 3
    return jax.shard_map(local, mesh=mesh, in_specs=in_specs, out_specs=out_specs, check_vma=False)
```
